32 devices in a mesh: row: 8 (over z, x), col: 4 (over y, core).
Axes of the slice: x: 2, y: 2, z: 4, core: 2. Of those that a mesh axis runs over, the one named last changes fastest.
Arguments:
- affinity: bfloat16 [32768, 8192], P('row', 'col'), may hold values from -250 to 250
- seed_values: int32 [16], replicated, may hold values from 0 to 1073741823
- sku_ids: int32 [8192], P('col'), may hold values from 0 to 8191, each once
Outputs:
- range_basis: float32 [16, 32768], P(None, ('row', 'col'))
- range_factor: float32 [16, 16], replicated
The draws below stay inside these ranges and needn't reach their ends.
All inputs are finite; a program needn't handle non-finite values.
Results may differ from the reference program's by a relative error of at most 0.0046.
Values may be sent and summed in bfloat16 or wider, within the bound.
A program may use at most 64 MiB of HBM per device.

```python
import math
import jax
import jax.numpy as jnp
from jax import lax

N = 8192
K = 16
ITERS = 2
ROWS = 32768


def draw_affinity(key, part):
    key_base = jax.random.fold_in(key, 11)
    key_rows = jax.random.fold_in(key, 12)
    key_cols = jax.random.fold_in(key, 13)
    position = jnp.arange(ROWS, dtype=jnp.float32)[:, None] / ROWS
    base = jax.random.normal(key_base, (ROWS, N), jnp.float32)
    trend = jnp.exp(math.log(3.0) * position)
    row_scale = jnp.exp(jax.random.uniform(key_rows, (ROWS, 1), jnp.float32, math.log(0.3), math.log(3.0)))
    col_scale = jnp.exp(jax.random.uniform(key_cols, (1, N), jnp.float32, math.log(0.5), math.log(2.0)))
    return (base * trend * row_scale * col_scale).astype(jnp.bfloat16)


def place_ends(result, key, smallest, top_value):
    place = [jax.random.randint(jax.random.fold_in(key, axis), (), 0, length) for axis, length in enumerate(result.shape)]
    longest = result.shape.index(max(result.shape))
    neighbour = place[:longest] + [(place[longest] + 1) % result.shape[longest]] + place[longest + 1:]
    return result.at[tuple(place)].set(smallest).at[tuple(neighbour)].set(top_value)


def setup_inputs(seed: int = 0) -> dict:
    keys = jax.random.split(jax.random.key(seed), 4)
    return {
        "affinity": draw_affinity(jax.random.fold_in(keys[3], 71), 0),
        "seed_values": place_ends(jax.random.randint(keys[1], (K,), 0, 1073741824), jax.random.fold_in(keys[1], 1), 0, 1073741823).astype(jnp.int32),
        "sku_ids": jax.random.permutation(keys[2], N).astype(jnp.int32),
    }


mix_first = -2048144789
mix_second = -1028477387
golden = -1640531535
salt_value = 1540483477

def shifted(value, amount):
    return lax.shift_right_logical(value, jnp.full(value.shape, amount, jnp.int32))

def scramble(value):
    value = jnp.bitwise_xor(value, shifted(value, 16))
    value = value * jnp.int32(mix_first)
    value = jnp.bitwise_xor(value, shifted(value, 13))
    value = value * jnp.int32(mix_second)
    return jnp.bitwise_xor(value, shifted(value, 16))

def test_matrix(seed_values, sku_ids, total_columns):
    first = scramble(jnp.bitwise_xor(seed_values[:, None], sku_ids[None, :] * jnp.int32(golden)))
    second = scramble(jnp.bitwise_xor(first, jnp.int32(salt_value)))
    uniform_a = (shifted(first, 9) + 1).astype(jnp.float32) / 8388608.0
    uniform_b = (shifted(second, 9) + 1).astype(jnp.float32) / 8388608.0
    gauss = jnp.sqrt(-2.0 * jnp.log(uniform_a)) * jnp.cos(6.283185307179586 * uniform_b)
    return (gauss / math.sqrt(total_columns)).astype(jnp.bfloat16)

def project(left, affinity):
    return lax.dot_general(left.astype(jnp.float32), affinity.astype(jnp.float32), (((1,), (1,)), ((), ())), preferred_element_type=jnp.float32)

def lower_solve(lower, right):
    return lax.linalg.triangular_solve(lower, right, left_side=True, lower=True)

def reference(affinity, seed_values, sku_ids):
    omega = test_matrix(seed_values, sku_ids, N)
    sketch = project(omega, affinity)
    for repeat in range(ITERS + 1):
        gram = jnp.dot(sketch.astype(jnp.float32), sketch.T.astype(jnp.float32), precision=lax.Precision.HIGHEST, preferred_element_type=jnp.float32)
        lower = jnp.linalg.cholesky(gram)
        ortho = lower_solve(lower, sketch)
        if repeat < ITERS:
            back = jnp.dot(ortho.astype(jnp.bfloat16).astype(jnp.float32), affinity.astype(jnp.float32), preferred_element_type=jnp.float32)
            sketch = project(back.astype(jnp.bfloat16), affinity) * (1.0 / math.sqrt(N))
    scale = math.sqrt(ROWS)
    return (ortho * scale, lower.T / scale)
```

```python
import functools
import math

import jax
import jax.numpy as jnp
from jax import lax
from jax.experimental import pallas as pl
from jax.experimental.pallas import tpu as pltpu
from jax.sharding import PartitionSpec as P

ITERS = 2
SUB = 2
DEPTH = 4
TASKS = ((0, 1, 2), (3, 4, 5), (6, 7))
HIGHEST = lax.Precision.HIGHEST
MESH = pl.DeviceIdType.MESH

mix_first = -2048144789
mix_second = -1028477387
golden = -1640531535
salt_value = 1540483477


def shifted(value, amount):
    return lax.shift_right_logical(value, jnp.full(value.shape, amount, jnp.int32))


def scramble(value):
    value = jnp.bitwise_xor(value, shifted(value, 16))
    value = value * jnp.int32(mix_first)
    value = jnp.bitwise_xor(value, shifted(value, 13))
    value = value * jnp.int32(mix_second)
    return jnp.bitwise_xor(value, shifted(value, 16))


def test_matrix(seeds, skus, total_columns):
    first = scramble(jnp.bitwise_xor(seeds, skus * jnp.int32(golden)))
    second = scramble(jnp.bitwise_xor(first, jnp.int32(salt_value)))
    uniform_a = (shifted(first, 9) + 1).astype(jnp.float32) / 8388608.0
    uniform_b = (shifted(second, 9) + 1).astype(jnp.float32) / 8388608.0
    gauss = jnp.sqrt(-2.0 * jnp.log(uniform_a)) * jnp.cos(6.283185307179586 * uniform_b)
    return (gauss / math.sqrt(total_columns)).astype(jnp.bfloat16)


def factorize(gram):
    count = gram.shape[0]
    rows = lax.broadcasted_iota(jnp.int32, (count, count), 0)
    cols = lax.broadcasted_iota(jnp.int32, (count, count), 1)
    left = gram
    right = (rows == cols).astype(jnp.float32)
    for j in range(count):
        pivot = left[j : j + 1, j : j + 1]
        inv = lax.rsqrt(pivot)
        inv = inv * (1.5 - 0.5 * (pivot * inv) * inv)
        left_row = left[j : j + 1, :] * inv
        right_row = right[j : j + 1, :] * inv
        factor = left[:, j : j + 1] * inv
        left = jnp.where(rows == j, left_row, jnp.where(rows > j, left - factor * left_row, left))
        right = jnp.where(rows == j, right_row, jnp.where(rows > j, right - factor * right_row, right))
    return jnp.where(rows <= cols, left, 0.0), right


def kernel(
    dims,
    slab_hbm, seed_hbm, sku_hbm,
    basis_ref, factor_ref,
    slab, slab_t, seed_ref, sku_ref, x_ref, acc, part, half_recv, y_sum, fin_part, fin_recv, fin_sum, fin_y,
    s_ref, lhs, zacc, zpart, zrecv, back,
    gsend_row, grecv_row, grecv_col, gcol, gram_part,
    load_sem, a_send_sem, a_recv_sem, y_send_sem, y_recv_sem, f_send_sem, f_recv_sem, fy_send_sem, fy_recv_sem,
    s_send_sem, s_recv_sem, z_send_sem, z_recv_sem, b_send_sem, b_recv_sem, g_send_sem, g_recv_sem,
    c_send_sem, c_recv_sem,
):
    R, C, K, piece, width, base, H, inv_root, scale = dims
    ow = width // H
    me_r = lax.axis_index("row")
    me_c = lax.axis_index("col")

    Y = C // 2
    core, me_y = lax.rem(me_c, 2), me_c // 2
    partner = me_y * 2 + (1 - core)

    flip = me_r // (R // 2)
    fr = me_r + flip * (R - 1 - 2 * me_r)
    is_owner = fr >= base
    mine_h = fr - base

    def unflip(row):
        return row + flip * (R - 1 - 2 * row)

    def block(k):
        if k == H - 1:
            near = jnp.maximum(mine_h, 0)
        else:
            near = (H - 1 - k) - (mine_h >= H - 1 - k).astype(jnp.int32)
        return unflip(base + near) - base

    def arrival(k):
        if k == 0:
            near = jnp.maximum(mine_h, 0)
        else:
            near = (k - 1) + (mine_h <= k - 1).astype(jnp.int32)
        return unflip(base + near) - base

    def listener(k):
        return unflip((R - 1 - k) - (fr >= R - 1 - k).astype(jnp.int32))

    def y_peer(k):
        return lax.rem(me_y + k, Y) * 2 + core

    def col_peer_of(k):
        return (1 - core) * Y + k if k < Y else core * Y + k - Y

    def row_peer(k):
        return lax.rem(me_r + k, R)

    def row_from(k):
        return lax.rem(me_r + (R - k), R)

    span = piece // SUB
    n_load = C * SUB

    def load(i):
        start = col_peer_of(i // SUB) * piece + (i % SUB) * span
        return pltpu.make_async_copy(
            slab_hbm.at[pl.ds(pl.multiple_of(start, span), span), :],
            slab.at[i // SUB, pl.ds((i % SUB) * span, span), :],
            load_sem.at[i],
        )

    seed_copy = pltpu.make_async_copy(seed_hbm, seed_ref, load_sem.at[n_load])
    sku_copy = pltpu.make_async_copy(sku_hbm, sku_ref, load_sem.at[n_load + 1])
    seed_copy.start()
    sku_copy.start()
    for i in range(min(DEPTH, n_load)):
        load(i).start()

    barrier = pltpu.get_barrier_semaphore()
    for k in range(1, R):
        pl.semaphore_signal(barrier, inc=1, device_id={"row": row_peer(k)}, device_id_type=MESH)
    for k in range(1, C):
        pl.semaphore_signal(barrier, inc=1, device_id={"col": lax.rem(me_c + k, C)}, device_id_type=MESH)

    seed_copy.wait()
    sku_copy.wait()
    index = lax.broadcasted_iota(jnp.int32, (K, width), 0)
    seeds = jnp.zeros((K, width), jnp.int32)
    for k in range(K):
        seeds = jnp.where(index == k, seed_ref[k], seeds)
    x_ref[...] = test_matrix(seeds, jnp.broadcast_to(sku_ref[...], (K, width)), width * C)

    def flip_task(i):
        here = slice((i % SUB) * span, (i % SUB + 1) * span)
        slab_t[i // SUB, :, here] = slab[i // SUB, here, :].T

    pending = []

    def col_copy(src, dst, send, recv, target):
        return pltpu.make_async_remote_copy(
            src_ref=src, dst_ref=dst, send_sem=send, recv_sem=recv,
            device_id={"col": lax.rem(target, C)}, device_id_type=MESH,
        )

    def row_copy(src, dst, send, recv, row):
        return pltpu.make_async_remote_copy(
            src_ref=src, dst_ref=dst, send_sem=send, recv_sem=recv,
            device_id={"row": row}, device_id_type=MESH,
        )

    def position(c):
        half = c // Y
        same = 1 - (half + core - 2 * half * core)
        return lax.rem(c, Y) + Y * same

    def half_copy(it, q):
        return col_copy(part.at[it, q], half_recv.at[it, q], a_send_sem.at[it, q], a_recv_sem.at[it, q], partner)

    def send_half(it, q):
        half_copy(it, q).start()
        pending.append(half_copy(it, q))

    def send_y(it, q, value):
        half_copy(it, q).wait_recv()
        y_sum[it, q, me_y] = value + half_recv[it, q]
        for k in range(1, Y):
            copy = col_copy(
                y_sum.at[it, q, me_y], y_sum.at[it, q, me_y],
                y_send_sem.at[it, q, k], y_recv_sem.at[it, q, k], y_peer(k),
            )
            copy.start()
            pending.append(copy)

    def square(value):
        return lax.dot_general(
            value, value, (((1,), (1,)), ((), ())), precision=HIGHEST, preferred_element_type=jnp.float32
        )

    def gram_copy(it, row, source):
        return row_copy(
            gsend_row.at[it], grecv_row.at[it, source], g_send_sem.at[it, row], g_recv_sem.at[it, source], row
        )

    def z_copy(it, h, source):
        return row_copy(
            zpart.at[it, h], zrecv.at[it, source], z_send_sem.at[it, h], z_recv_sem.at[it, source], base + h
        )

    def back_copy(it, row, h):
        return row_copy(
            back.at[it, h], back.at[it, h], b_send_sem.at[it, row], b_recv_sem.at[it, h], row
        )

    def gather_project(it):
        for k in range(H):
            h = arrival(k)
            if k == 0:
                @pl.when(jnp.logical_not(is_owner))
                def _():
                    back_copy(it, me_r, h).wait_recv()
            else:
                back_copy(it, me_r, h).wait_recv()
            rows = pl.ds(pl.multiple_of(h * ow, ow), ow)

            def product(slot, h=h, rows=rows):
                return jnp.dot(back[it, h], slab_t[slot, rows, :], preferred_element_type=jnp.float32)

            if k < H - 1:
                for slot in range(C):
                    value = product(slot)
                    acc[slot] = value if k == 0 else acc[slot] + value
        return lambda slot: acc[slot] + product(slot)

    for it in range(ITERS):
        if it == 0:
            for i in range(n_load):
                k, sub = i // SUB, i % SUB
                here = slice(sub * span, (sub + 1) * span)
                load(i).wait()
                if i + DEPTH < n_load:
                    load(i + DEPTH).start()
                value = lax.dot_general(
                    x_ref[...], slab[k, here, :], (((1,), (1,)), ((), ())), preferred_element_type=jnp.float32
                )
                if k < Y:
                    part[it, k, :, here] = value
                    if i == Y * SUB - 1:
                        pl.semaphore_wait(barrier, (R - 1) + (C - 1))
                        for q in range(Y):
                            send_half(it, q)
                else:
                    acc[k, :, here] = value
                    if sub == SUB - 1:
                        send_y(it, k - Y, acc[k])
        else:
            last = gather_project(it - 1)
            for q in range(Y):
                part[it, q] = last(q)
                send_half(it, q)
            for q in range(Y):
                value = last(Y + q)
                send_y(it, q, value)
        if it == 0:
            for i in TASKS[0]:
                flip_task(i)
        for q in range(C):
            at = Y + q if q < Y else q - Y
            if q < Y:
                c = core * Y + q
                for k in range(1, Y):
                    source = lax.rem(me_y + (Y - k), Y)
                    col_copy(
                        y_sum.at[it, q, source], y_sum.at[it, q, source],
                        y_send_sem.at[it, q, k], y_recv_sem.at[it, q, k], y_peer(k),
                    ).wait_recv()
                value = y_sum[it, q, 0]
                for y in range(1, Y):
                    value = value + y_sum[it, q, y]
                if it > 0:
                    value = value * inv_root
                s_ref[it, c] = value
                copy = col_copy(
                    s_ref.at[it, c], s_ref.at[it, c], s_send_sem.at[it, q], s_recv_sem.at[it, q], partner
                )
                copy.start()
                pending.append(copy)
            else:
                c = (1 - core) * Y + q - Y
                col_copy(
                    s_ref.at[it, c], s_ref.at[it, c], s_send_sem.at[it, q - Y], s_recv_sem.at[it, q - Y], partner
                ).wait_recv()
                value = s_ref[it, c]
            high = value.astype(jnp.bfloat16)
            low = (value - high.astype(jnp.float32)).astype(jnp.bfloat16)
            lhs[:K, :] = high
            lhs[K:, :] = low
            if q < C - 1 or ow % 128:
                product = jnp.dot(lhs[...], slab[at], preferred_element_type=jnp.float32)
                product = product[:K] + product[K:]
                zacc[...] = product if q == 0 else zacc[...] + product
            gram_part[it, c] = square(value)
        gram = gram_part[it, 0]
        for c in range(1, C):
            gram = gram + gram_part[it, c]

        gsend_row[it] = gram
        for k in range(H - 1):
            gram_copy(it, base + block(k), me_r).start()

        @pl.when(jnp.logical_not(is_owner))
        def _():
            gram_copy(it, base + block(H - 1), me_r).start()

        @pl.when(is_owner)
        def _():
            grecv_row[it, me_r] = gsend_row[it]

        if ow % 128:
            for h in range(H):
                zpart[it, h] = zacc[:, h * ow : (h + 1) * ow]
        for k in range(H):
            h = block(k)
            if ow % 128 == 0:
                cols = pl.ds(pl.multiple_of(h * ow, ow), ow)
                product = jnp.dot(lhs[...], slab[Y - 1, :, cols], preferred_element_type=jnp.float32)
                zpart[it, h] = zacc[:, cols] + product[:K] + product[K:]
            if k < H - 1:
                z_copy(it, h, me_r).start()
            else:
                @pl.when(jnp.logical_not(is_owner))
                def _():
                    z_copy(it, h, me_r).start()

        if it == 0:
            for i in TASKS[1]:
                flip_task(i)

        @pl.when(is_owner)
        def _():
            for k in range(1, R):
                gram_copy(it, me_r, row_from(k)).wait_recv()
            total = grecv_row[it, 0]
            for r in range(1, R):
                total = total + grecv_row[it, r]
            _, inverse = factorize(total)
            own = me_r - base
            total = zpart[it, own]
            for k in range(1, R):
                source = row_from(k)
                z_copy(it, own, source).wait_recv()
                total = total + zrecv[it, source]
            back[it, own] = jnp.dot(
                inverse, total, precision=HIGHEST, preferred_element_type=jnp.float32
            ).astype(jnp.bfloat16)
            for k in range(R - 1):
                back_copy(it, listener(k), own).start()

        if it == 0:
            for i in TASKS[2]:
                flip_task(i)

    last = gather_project(ITERS - 1)
    inner = []
    for y in range(Y):
        fin_part[y] = last(position(y * 2 + (1 - core)))
        copy = col_copy(fin_part.at[y], fin_recv.at[y], f_send_sem.at[y], f_recv_sem.at[y], partner)
        copy.start()
        inner.append(copy)
    for k in list(range(1, Y)) + [0]:
        y = lax.rem(me_y + k, Y)
        fin_sum[k] = last(position(y * 2 + core))
    for copy in inner:
        copy.wait_recv()
    pending += inner
    outer = []
    for k in range(1, Y):
        y = lax.rem(me_y + k, Y)
        fin_sum[k] = fin_sum[k] + fin_recv[y]
        copy = col_copy(fin_sum.at[k], fin_y.at[k], fy_send_sem.at[k], fy_recv_sem.at[k], y_peer(k))
        copy.start()
        outer.append(copy)
    own = fin_sum[0] + fin_recv[me_y]
    for k, copy in enumerate(outer):
        copy.wait_recv()
        own = own + fin_y[k + 1]
    pending += outer
    own = own * inv_root
    gcol[...] = square(own)
    copies = []
    for k in range(1, C):
        copy = col_copy(gcol, grecv_col.at[me_c], c_send_sem.at[k], c_recv_sem.at[k], me_c + k)
        copy.start()
        copies.append(copy)
    grecv_col[me_c] = gcol[...]
    for k in range(1, C):
        source = lax.rem(me_c + (C - k), C)
        col_copy(gcol, grecv_col.at[source], c_send_sem.at[k], c_recv_sem.at[k], me_c + k).wait_recv()
    pending += copies
    gram = grecv_col[0]
    for c in range(1, C):
        gram = gram + grecv_col[c]
    gsend_row[ITERS] = gram
    for k in list(range(R // 2, R)) + list(range(1, R // 2)):
        copy = gram_copy(ITERS, row_peer(k), me_r)
        copy.start()
        pending.append(copy)
    grecv_row[ITERS, me_r] = gram

    for copy in pending:
        copy.wait_send()
    for it in range(ITERS):
        for k in range(H - 1):
            gram_copy(it, base + block(k), me_r).wait_send()
            z_copy(it, block(k), me_r).wait_send()

        @pl.when(jnp.logical_not(is_owner))
        def _():
            gram_copy(it, base + block(H - 1), me_r).wait_send()
            z_copy(it, block(H - 1), me_r).wait_send()

        @pl.when(is_owner)
        def _():
            for k in range(R - 1):
                back_copy(it, listener(k), me_r - base).wait_send()

    for k in range(1, R):
        gram_copy(ITERS, me_r, row_from(k)).wait_recv()
    gram = grecv_row[ITERS, 0]
    for r in range(1, R):
        gram = gram + grecv_row[ITERS, r]
    upper, inverse = factorize(gram)
    ortho = jnp.dot(inverse, own, precision=HIGHEST, preferred_element_type=jnp.float32)
    basis_ref[...] = ortho * scale
    factor_ref[...] = upper / scale


def body(affinity, seed_values, sku_ids):
    R, C = lax.axis_size("row"), lax.axis_size("col")
    K = seed_values.shape[0]
    rows, width = affinity.shape
    piece, Y = rows // C, C // 2
    base, H = R // 4, R // 2
    ow = width // H
    dims = (R, C, K, piece, width, base, H, 1.0 / math.sqrt(width * C), math.sqrt(rows * R))
    f32, bf16 = jnp.float32, jnp.bfloat16
    dma = pltpu.SemaphoreType.DMA
    vmem = pl.BlockSpec(memory_space=pltpu.VMEM)
    return pl.pallas_call(
        functools.partial(kernel, dims),
        out_shape=(
            jax.ShapeDtypeStruct((K, piece), f32),
            jax.ShapeDtypeStruct((K, K), f32),
        ),
        in_specs=[pl.BlockSpec(memory_space=pl.ANY)] * 3,
        out_specs=(vmem, vmem),
        scratch_shapes=[
            pltpu.VMEM((C, piece, width), bf16),
            pltpu.VMEM((C, width, piece), bf16),
            pltpu.SMEM((K,), jnp.int32),
            pltpu.VMEM((1, width), jnp.int32),
            pltpu.VMEM((K, width), bf16),
            pltpu.VMEM((C, K, piece), f32),
            pltpu.VMEM((ITERS, Y, K, piece), f32),
            pltpu.VMEM((ITERS, Y, K, piece), f32),
            pltpu.VMEM((ITERS, Y, Y, K, piece), f32),
            pltpu.VMEM((Y, K, piece), f32),
            pltpu.VMEM((Y, K, piece), f32),
            pltpu.VMEM((Y, K, piece), f32),
            pltpu.VMEM((Y, K, piece), f32),
            pltpu.VMEM((ITERS, C, K, piece), f32),
            pltpu.VMEM((2 * K, piece), bf16),
            pltpu.VMEM((K, width), f32),
            pltpu.VMEM((ITERS, H, K, ow), f32),
            pltpu.VMEM((ITERS, R, K, ow), f32),
            pltpu.VMEM((ITERS, H, K, ow), bf16),
            pltpu.VMEM((ITERS + 1, K, K), f32),
            pltpu.VMEM((ITERS + 1, R, K, K), f32),
            pltpu.VMEM((C, K, K), f32),
            pltpu.VMEM((K, K), f32),
            pltpu.VMEM((ITERS, C, K, K), f32),
            dma((C * SUB + 2,)),
            dma((ITERS, Y)), dma((ITERS, Y)),
            dma((ITERS, Y, Y)), dma((ITERS, Y, Y)),
            dma((Y,)), dma((Y,)),
            dma((Y,)), dma((Y,)),
            dma((ITERS, Y)), dma((ITERS, Y)),
            dma((ITERS, H)), dma((ITERS, R)),
            dma((ITERS, R)), dma((ITERS, H)),
            dma((ITERS + 1, R)), dma((ITERS + 1, R)),
            dma((C,)), dma((C,)),
        ],
        compiler_params=pltpu.CompilerParams(
            collective_id=0, has_side_effects=True, vmem_limit_bytes=60 * 1024 * 1024
        ),
    )(affinity, seed_values, sku_ids[None, :])


def solution(mesh):
    placed = (P("row", "col"), P(), P("col"))
    return jax.shard_map(
        body, mesh=mesh, in_specs=placed, out_specs=(P(None, ("row", "col")), P()), check_vma=False
    )
```

```python
import functools
import math

import jax
import jax.numpy as jnp
from jax import lax
from jax.experimental import pallas as pl
from jax.experimental.pallas import tpu as pltpu
from jax.sharding import PartitionSpec as P

ITERS = 2
SUB = 2
DEPTH = 4
LANES = 128
TASKS = ((0, 1), (2, 3, 4), (5, 6, 7))
HIGHEST = lax.Precision.HIGHEST
MESH = pl.DeviceIdType.MESH

mix_first = -2048144789
mix_second = -1028477387
golden = -1640531535
salt_value = 1540483477


def shifted(value, amount):
    return lax.shift_right_logical(value, jnp.full(value.shape, amount, jnp.int32))


def scramble(value):
    value = jnp.bitwise_xor(value, shifted(value, 16))
    value = value * jnp.int32(mix_first)
    value = jnp.bitwise_xor(value, shifted(value, 13))
    value = value * jnp.int32(mix_second)
    return jnp.bitwise_xor(value, shifted(value, 16))


def test_matrix(seeds, skus, total_columns):
    first = scramble(jnp.bitwise_xor(seeds, skus * jnp.int32(golden)))
    second = scramble(jnp.bitwise_xor(first, jnp.int32(salt_value)))
    uniform_a = (shifted(first, 9) + 1).astype(jnp.float32) / 8388608.0
    uniform_b = (shifted(second, 9) + 1).astype(jnp.float32) / 8388608.0
    gauss = jnp.sqrt(-2.0 * jnp.log(uniform_a)) * jnp.cos(6.283185307179586 * uniform_b)
    return (gauss / math.sqrt(total_columns)).astype(jnp.bfloat16)


def factorize(gram):
    count = gram.shape[0]
    rows = lax.broadcasted_iota(jnp.int32, (count, count), 0)
    cols = lax.broadcasted_iota(jnp.int32, (count, count), 1)
    left = gram
    right = (rows == cols).astype(jnp.float32)
    for j in range(count):
        pivot = left[j : j + 1, j : j + 1]
        inv = lax.rsqrt(pivot)
        inv = inv * (1.5 - 0.5 * (pivot * inv) * inv)
        left_row = left[j : j + 1, :] * inv
        right_row = right[j : j + 1, :] * inv
        factor = left[:, j : j + 1] * inv
        left = jnp.where(rows == j, left_row, jnp.where(rows > j, left - factor * left_row, left))
        right = jnp.where(rows == j, right_row, jnp.where(rows > j, right - factor * right_row, right))
    return jnp.where(rows <= cols, left, 0.0), right


def repeat(start, stop, step):
    if stop - start <= 64:
        for k in range(start, stop):
            step(k)
    else:
        lax.fori_loop(start, stop, lambda k, _: (step(k), 0)[1], 0)


def kernel(
    dims,
    slab_hbm, seed_hbm, sku_hbm,
    basis_ref, factor_ref,
    slab, slab_t, seed_ref, sku_ref, x_ref, acc, part, half_recv, y_send, y_sum,
    fin_part, fin_recv, fin_send, fin_y, s_ref, lhs, zacc, zpart, zrecv, block_ref, back,
    gsend, grecv, fsend, frecv,
    load_sem, a_send_sem, a_recv_sem, y_send_sem, y_recv_sem, f_send_sem, f_recv_sem, fy_send_sem, fy_recv_sem,
    s_send_sem, s_recv_sem, z_send_sem, z_recv_sem, b_send_sem, b_recv_sem, g_send_sem, g_recv_sem,
    c_send_sem, c_recv_sem,
):
    R, C, K, piece, width, base, H, W, inv_root, scale = dims
    wave = width // W
    bw = wave // H
    me_r = lax.axis_index("row")
    me_c = lax.axis_index("col")
    me = me_r * C + me_c

    Y = C // 2
    core, me_y = lax.rem(me_c, 2), me_c // 2
    other = 1 - core
    partner = me_y * 2 + other

    flip = me_r // (R // 2)
    is_owner = jnp.logical_and(me_r >= base, me_r < base + H)

    def far(k):
        return (H - 1 - k) + flip * (2 * k - H + 1)

    def far_row(k):
        return (R - 1 - k) + flip * (2 * k - R + 1)

    span = piece // SUB
    n_load = C * SUB

    def load(i):
        k = i // SUB
        start = ((other * Y + k) if k < Y else (core * Y + k - Y)) * piece + (i % SUB) * span
        return pltpu.make_async_copy(
            slab_hbm.at[pl.ds(pl.multiple_of(start, span), span), :],
            slab.at[k, pl.ds((i % SUB) * span, span), :],
            load_sem.at[i],
        )

    seed_copy = pltpu.make_async_copy(seed_hbm, seed_ref, load_sem.at[n_load])
    sku_copy = pltpu.make_async_copy(sku_hbm, sku_ref, load_sem.at[n_load + 1])
    seed_copy.start()
    sku_copy.start()
    for i in range(min(DEPTH, n_load)):
        load(i).start()

    def peer(k):
        index = lax.rem(me + k, R * C)
        return {"row": index // C, "col": lax.rem(index, C)}

    barrier = pltpu.get_barrier_semaphore()

    def greet(k):
        pl.semaphore_signal(barrier, inc=1, device_id=peer(k), device_id_type=MESH)

    repeat(1, R * C, greet)

    seed_copy.wait()
    sku_copy.wait()
    index = lax.broadcasted_iota(jnp.int32, (K, width), 0)
    seeds = jnp.zeros((K, width), jnp.int32)
    for k in range(K):
        seeds = jnp.where(index == k, seed_ref[k], seeds)
    x_ref[...] = test_matrix(seeds, jnp.broadcast_to(sku_ref[...], (K, width)), width * C)

    def turn(i):
        here = slice((i % SUB) * span, (i % SUB + 1) * span)
        slab_t[i // SUB, :, here] = slab[i // SUB, here, :].T

    pending = []

    def remote(src, dst, send, recv, row, col):
        return pltpu.make_async_remote_copy(
            src_ref=src, dst_ref=dst, send_sem=send, recv_sem=recv,
            device_id={"row": row, "col": col}, device_id_type=MESH,
        )

    def go(copy):
        copy.start()
        pending.append(copy)

    def position(c):
        half = c // Y
        same = 1 - (half + core - 2 * half * core)
        return lax.rem(c, Y) + Y * same

    def swap(it, slot):
        there = (slot + Y) % C
        return remote(
            part.at[it, slot], half_recv.at[it, there], a_send_sem.at[it, slot], a_recv_sem.at[it, there],
            me_r, partner,
        )

    def swapped(it, slot):
        return remote(
            part.at[it, slot], half_recv.at[it, slot], a_send_sem.at[it, slot], a_recv_sem.at[it, slot],
            me_r, partner,
        )

    def cross(it, q, k):
        y = lax.rem(me_y + k, Y)
        return remote(
            y_send.at[it, q], y_sum.at[it, q, me_y], y_send_sem.at[it, q, k], y_recv_sem.at[it, q, me_y],
            me_r, y * 2 + other,
        )

    def crossed(it, q, y):
        return remote(
            y_send.at[it, q], y_sum.at[it, q, y], y_send_sem.at[it, q, 0], y_recv_sem.at[it, q, y], me_r, partner
        )

    def square(value):
        return lax.dot_general(
            value, value, (((1,), (1,)), ((), ())), precision=HIGHEST, preferred_element_type=jnp.float32
        )

    def gram_copy(it, h, c, source):
        return remote(
            gsend.at[it], grecv.at[it, source], g_send_sem.at[it, h, c], g_recv_sem.at[it, source],
            base + h, me_y * 2 + c,
        )

    def z_copy(it, w, h, source):
        return remote(
            zpart.at[it, w, h], zrecv.at[it, w, source], z_send_sem.at[it, w, h], z_recv_sem.at[it, w, source],
            base + h, partner,
        )

    def back_copy(it, w, row, h):
        cols = pl.ds(pl.multiple_of(h * bw, bw), bw)
        return remote(
            block_ref.at[it, w], back.at[it, w, :, cols], b_send_sem.at[it, w, row], b_recv_sem.at[it, w, h],
            row, partner,
        )

    def gathered(it):
        def product(w, slot):
            rows = slice(w * wave, (w + 1) * wave)
            return jnp.dot(back[it, w], slab_t[slot, rows, :], preferred_element_type=jnp.float32)

        for w in range(W):
            for h in range(H):
                back_copy(it, w, me_r, h).wait_recv()
            if w < W - 1:
                for slot in range(C):
                    value = product(w, slot)
                    acc[slot] = value if w == 0 else acc[slot] + value
        if W == 1:
            return lambda slot: product(0, slot)
        return lambda slot: acc[slot] + product(W - 1, slot)

    for it in range(ITERS):
        def hand_over(q):
            swapped(it, Y + q).wait_recv()
            y_send[it, q] = part[it, Y + q] + half_recv[it, Y + q]
            for k in range(1, Y):
                go(cross(it, q, k))

        if it == 0:
            for i in range(n_load):
                k, sub = i // SUB, i % SUB
                here = slice(sub * span, (sub + 1) * span)
                load(i).wait()
                if i + DEPTH < n_load:
                    load(i + DEPTH).start()
                part[it, k, :, here] = lax.dot_general(
                    x_ref[...], slab[k, here, :], (((1,), (1,)), ((), ())), preferred_element_type=jnp.float32
                )
                if i == Y * SUB - 1:
                    pl.semaphore_wait(barrier, R * C - 1)
                    for slot in range(Y):
                        go(swap(it, slot))
                if k >= Y and sub == SUB - 1:
                    go(swap(it, k))
                    hand_over(k - Y)
            for i in TASKS[0]:
                turn(i)
        else:
            last = gathered(it - 1)
            for slot in range(C):
                part[it, slot] = last(slot)
                go(swap(it, slot))
            for q in range(Y):
                hand_over(q)
        for q in range(Y):
            swapped(it, q).wait_recv()
            y_sum[it, q, me_y] = part[it, q] + half_recv[it, q]

        gram = None
        for slot in range(C):
            if slot < Y:
                for k in range(1, Y):
                    crossed(it, slot, lax.rem(me_y + (Y - k), Y)).wait_recv()
                value = y_sum[it, slot, 0]
                for y in range(1, Y):
                    value = value + y_sum[it, slot, y]
                if it > 0:
                    value = value * inv_root
                s_ref[it, slot] = value
                go(
                    remote(
                        s_ref.at[it, slot], s_ref.at[it, Y + slot], s_send_sem.at[it, slot], s_recv_sem.at[it, slot],
                        me_r, partner,
                    )
                )
                gram = square(value) if slot == 0 else gram + square(value)
                if slot == Y - 1:
                    gsend[it] = gram
                    for k in range(H):
                        h = far(k)
                        go(gram_copy(it, h, other, me_r * 2 + core))

                        @pl.when(me_r != base + h)
                        def _():
                            gram_copy(it, h, core, me_r * 2 + core).start()

                    @pl.when(is_owner)
                    def _():
                        grecv[it, me_r * 2 + core] = gsend[it]
            else:
                remote(
                    s_ref.at[it, slot - Y], s_ref.at[it, slot],
                    s_send_sem.at[it, slot - Y], s_recv_sem.at[it, slot - Y], me_r, partner,
                ).wait_recv()
                value = s_ref[it, slot]
            high = value.astype(jnp.bfloat16)
            low = (value - high.astype(jnp.float32)).astype(jnp.bfloat16)
            lhs[:K, :] = high
            lhs[K:, :] = low
            if slot < C - 1:
                product = jnp.dot(lhs[...], slab[slot], preferred_element_type=jnp.float32)
                product = product[:K] + product[K:]
                zacc[...] = product if slot == 0 else zacc[...] + product
        for w in range(W):
            cols = slice(w * wave, (w + 1) * wave)
            product = jnp.dot(lhs[...], slab[C - 1, :, cols], preferred_element_type=jnp.float32)
            product = zacc[:, cols] + product[:K] + product[K:]
            for h in range(H):
                zpart[it, w, h] = product[:, h * bw : (h + 1) * bw]
            for k in range(H):
                go(z_copy(it, w, far(k), me_r))

        if it == 0:
            for i in TASKS[1]:
                turn(i)

        @pl.when(is_owner)
        def _():
            gram_copy(it, me_r - base, core, me_r * 2 + other).wait_recv()
            for k in range(1, R):
                source = lax.rem(me_r + k, R) * 2
                gram_copy(it, me_r - base, core, source).wait_recv()
                gram_copy(it, me_r - base, core, source + 1).wait_recv()
            total = grecv[it, 0]
            for r in range(1, 2 * R):
                total = total + grecv[it, r]
            _, inverse = factorize(total)
            own = me_r - base
            for w in range(W):
                for r in range(R):
                    z_copy(it, w, own, r).wait_recv()
                total = zrecv[it, w, 0]
                for r in range(1, R):
                    total = total + zrecv[it, w, r]
                block_ref[it, w] = jnp.dot(
                    inverse, total, precision=HIGHEST, preferred_element_type=jnp.float32
                ).astype(jnp.bfloat16)
                for k in range(R):
                    back_copy(it, w, far_row(k), own).start()

        if it == 0:
            for i in TASKS[2]:
                turn(i)

    last = gathered(ITERS - 1)

    def to_partner(k):
        y = lax.rem(me_y + k, Y)
        return remote(
            fin_part.at[k], fin_recv.at[k], f_send_sem.at[k], f_recv_sem.at[k], me_r, partner
        ), y

    for k in list(range(1, Y)) + [0]:
        copy, y = to_partner(k)
        fin_part[k] = last(position(y * 2 + (core if k else other)))
        go(copy)
    for k in list(range(1, Y)) + [0]:
        y = lax.rem(me_y + k, Y)
        fin_send[k] = last(position(y * 2 + (other if k else core)))
    outer = []
    for k in range(1, Y):
        copy, y = to_partner(k)
        copy.wait_recv()
        fin_send[k] = fin_send[k] + fin_recv[k]
        copy = remote(
            fin_send.at[k], fin_y.at[k], fy_send_sem.at[k], fy_recv_sem.at[k], me_r, y * 2 + other
        )
        go(copy)
        outer.append(copy)
    to_partner(0)[0].wait_recv()
    own = fin_send[0] + fin_recv[0]
    for k, copy in enumerate(outer):
        copy.wait_recv()
        own = own + fin_y[k + 1]
    own = own * inv_root
    fsend[...] = square(own)

    def spread(k):
        return pltpu.make_async_remote_copy(
            src_ref=fsend, dst_ref=frecv.at[me], send_sem=c_send_sem.at[k],
            recv_sem=c_recv_sem.at[me], device_id=peer(k), device_id_type=MESH,
        )

    def collect(k):
        source = lax.rem(me + k, R * C)
        pltpu.make_async_remote_copy(
            src_ref=fsend, dst_ref=frecv.at[source], send_sem=c_send_sem.at[k],
            recv_sem=c_recv_sem.at[source], device_id=peer(k), device_id_type=MESH,
        ).wait_recv()

    repeat(1, R * C, lambda k: spread(k).start())
    frecv[me] = fsend[...]

    for copy in pending:
        copy.wait_send()
    for it in range(ITERS):
        for h in range(H):
            @pl.when(me_r != base + h)
            def _():
                gram_copy(it, h, core, me_r * 2 + core).wait_send()

        @pl.when(is_owner)
        def _():
            for w in range(W):
                for row in range(R):
                    back_copy(it, w, row, me_r - base).wait_send()

    repeat(1, R * C, collect)
    parts = [frecv[r] for r in range(8)]
    for r in range(8, R * C):
        parts[r % 8] = parts[r % 8] + frecv[r]
    while len(parts) > 1:
        parts = [a + b for a, b in zip(parts[::2], parts[1::2])]
    upper, inverse = factorize(parts[0])
    ortho = jnp.dot(inverse, own, precision=HIGHEST, preferred_element_type=jnp.float32)
    basis_ref[...] = ortho * scale
    factor_ref[...] = upper / scale
    repeat(1, R * C, lambda k: spread(k).wait_send())


def body(affinity, seed_values, sku_ids):
    R, C = lax.axis_size("row"), lax.axis_size("col")
    K = seed_values.shape[0]
    rows, width = affinity.shape
    piece, Y = rows // C, C // 2
    H = min(R // 2, width // LANES)
    W = 2 if width % (2 * H * LANES) == 0 else 1
    base, wave, bw = (R - H) // 2, width // W, width // W // H
    dims = (R, C, K, piece, width, base, H, W, 1.0 / math.sqrt(width * C), math.sqrt(rows * R))
    f32, bf16 = jnp.float32, jnp.bfloat16
    dma = pltpu.SemaphoreType.DMA
    vmem = pl.BlockSpec(memory_space=pltpu.VMEM)
    return pl.pallas_call(
        functools.partial(kernel, dims),
        out_shape=(
            jax.ShapeDtypeStruct((K, piece), f32),
            jax.ShapeDtypeStruct((K, K), f32),
        ),
        in_specs=[pl.BlockSpec(memory_space=pl.ANY)] * 3,
        out_specs=(vmem, vmem),
        scratch_shapes=[
            pltpu.VMEM((C, piece, width), bf16),
            pltpu.VMEM((C, width, piece), bf16),
            pltpu.SMEM((K,), jnp.int32),
            pltpu.VMEM((1, width), jnp.int32),
            pltpu.VMEM((K, width), bf16),
            pltpu.VMEM((C, K, piece), f32),
            pltpu.VMEM((ITERS, C, K, piece), f32),
            pltpu.VMEM((ITERS, C, K, piece), f32),
            pltpu.VMEM((ITERS, Y, K, piece), f32),
            pltpu.VMEM((ITERS, Y, Y, K, piece), f32),
            pltpu.VMEM((Y, K, piece), f32),
            pltpu.VMEM((Y, K, piece), f32),
            pltpu.VMEM((Y, K, piece), f32),
            pltpu.VMEM((Y, K, piece), f32),
            pltpu.VMEM((ITERS, C, K, piece), f32),
            pltpu.VMEM((2 * K, piece), bf16),
            pltpu.VMEM((K, width), f32),
            pltpu.VMEM((ITERS, W, H, K, bw), f32),
            pltpu.VMEM((ITERS, W, R, K, bw), f32),
            pltpu.VMEM((ITERS, W, K, bw), bf16),
            pltpu.VMEM((ITERS, W, K, wave), bf16),
            pltpu.VMEM((ITERS, K, K), f32),
            pltpu.VMEM((ITERS, 2 * R, K, K), f32),
            pltpu.VMEM((K, K), f32),
            pltpu.VMEM((R * C, K, K), f32),
            dma((C * SUB + 2,)),
            dma((ITERS, C)), dma((ITERS, C)),
            dma((ITERS, Y, Y)), dma((ITERS, Y, Y)),
            dma((Y,)), dma((Y,)),
            dma((Y,)), dma((Y,)),
            dma((ITERS, Y)), dma((ITERS, Y)),
            dma((ITERS, W, H)), dma((ITERS, W, R)),
            dma((ITERS, W, R)), dma((ITERS, W, H)),
            dma((ITERS, H, 2)), dma((ITERS, 2 * R)),
            dma((R * C,)), dma((R * C,)),
        ],
        compiler_params=pltpu.CompilerParams(
            collective_id=0, has_side_effects=True, vmem_limit_bytes=60 * 1024 * 1024
        ),
    )(affinity, seed_values, sku_ids[None, :])


def solution(mesh):
    placed = (P("row", "col"), P(), P("col"))
    return jax.shard_map(
        body, mesh=mesh, in_specs=placed, out_specs=(P(None, ("row", "col")), P()), check_vma=False
    )
```

```python
import functools
import math

import jax
import jax.numpy as jnp
from jax import lax
from jax.experimental import pallas as pl
from jax.experimental.pallas import tpu as pltpu
from jax.sharding import PartitionSpec as P

ITERS = 2
SUB = 2
DEPTH = 4
LANES = 128
TASKS = ((0, 1), (2, 3, 4), (5,), (6, 7))
HIGHEST = lax.Precision.HIGHEST
MESH = pl.DeviceIdType.MESH

mix_first = -2048144789
mix_second = -1028477387
golden = -1640531535
salt_value = 1540483477


def shifted(value, amount):
    return lax.shift_right_logical(value, jnp.full(value.shape, amount, jnp.int32))


def scramble(value):
    value = jnp.bitwise_xor(value, shifted(value, 16))
    value = value * jnp.int32(mix_first)
    value = jnp.bitwise_xor(value, shifted(value, 13))
    value = value * jnp.int32(mix_second)
    return jnp.bitwise_xor(value, shifted(value, 16))


def test_matrix(seeds, skus, total_columns):
    first = scramble(jnp.bitwise_xor(seeds, skus * jnp.int32(golden)))
    second = scramble(jnp.bitwise_xor(first, jnp.int32(salt_value)))
    uniform_a = (shifted(first, 9) + 1).astype(jnp.float32) / 8388608.0
    uniform_b = (shifted(second, 9) + 1).astype(jnp.float32) / 8388608.0
    gauss = jnp.sqrt(-2.0 * jnp.log(uniform_a)) * jnp.cos(6.283185307179586 * uniform_b)
    return (gauss / math.sqrt(total_columns)).astype(jnp.bfloat16)


def factorize(gram):
    count = gram.shape[0]
    rows = lax.broadcasted_iota(jnp.int32, (count, count), 0)
    cols = lax.broadcasted_iota(jnp.int32, (count, count), 1)
    left = gram
    right = (rows == cols).astype(jnp.float32)
    for j in range(count):
        pivot = left[j : j + 1, j : j + 1]
        inv = lax.rsqrt(pivot)
        inv = inv * (1.5 - 0.5 * (pivot * inv) * inv)
        left_row = left[j : j + 1, :] * inv
        right_row = right[j : j + 1, :] * inv
        factor = left[:, j : j + 1] * inv
        left = jnp.where(rows == j, left_row, jnp.where(rows > j, left - factor * left_row, left))
        right = jnp.where(rows == j, right_row, jnp.where(rows > j, right - factor * right_row, right))
    return jnp.where(rows <= cols, left, 0.0), right


def repeat(start, stop, step):
    if stop - start <= 64:
        for k in range(start, stop):
            step(k)
    else:
        lax.fori_loop(start, stop, lambda k, _: (step(k), 0)[1], 0)


def kernel(
    dims,
    slab_hbm, seed_hbm, sku_hbm,
    basis_ref, factor_ref,
    slab, slab_t, seed_ref, sku_ref, x_ref, acc, part, half_recv, y_send, y_sum,
    fin_part, fin_recv, fin_send, fin_y, s_ref, lhs, zacc, zpart, zrecv, block_ref, back,
    gsend, grecv, fsend, frecv,
    load_sem, send_sem, a_recv_sem, y_recv_sem, f_recv_sem, fy_recv_sem, s_recv_sem, z_recv_sem, b_recv_sem,
    g_recv_sem, c_recv_sem,
):
    R, C, K, piece, width, base, H, W, inv_root, scale = dims
    wave = width // W
    bw = wave // H
    me_r = lax.axis_index("row")
    me_c = lax.axis_index("col")
    me = me_r * C + me_c

    Y = C // 2
    core, me_y = lax.rem(me_c, 2), me_c // 2
    other = 1 - core
    partner = me_y * 2 + other

    flip = me_r // (R // 2)
    is_owner = jnp.logical_and(me_r >= base, me_r < base + H)

    def far(k):
        return (H - 1 - k) + flip * (2 * k - H + 1)

    def far_row(k):
        return (R - 1 - k) + flip * (2 * k - R + 1)

    span = piece // SUB
    n_load = C * SUB

    def load(i):
        k = i // SUB
        start = ((other * Y + k) if k < Y else (core * Y + k - Y)) * piece + (i % SUB) * span
        return pltpu.make_async_copy(
            slab_hbm.at[pl.ds(pl.multiple_of(start, span), span), :],
            slab.at[pl.ds(i * span, span), :],
            load_sem.at[i % DEPTH],
        )

    seed_copy = pltpu.make_async_copy(seed_hbm, seed_ref, load_sem.at[DEPTH])
    sku_copy = pltpu.make_async_copy(sku_hbm, sku_ref, load_sem.at[DEPTH + 1])
    seed_copy.start()
    sku_copy.start()
    for i in range(min(DEPTH, n_load)):
        load(i).start()

    def peer(k):
        index = lax.rem(me + k, R * C)
        return {"row": index // C, "col": lax.rem(index, C)}

    barrier = pltpu.get_barrier_semaphore()

    def greet(k):
        pl.semaphore_signal(barrier, inc=1, device_id=peer(k), device_id_type=MESH)

    repeat(1, R * C, greet)

    seed_copy.wait()
    sku_copy.wait()
    index = lax.broadcasted_iota(jnp.int32, (K, width), 0)
    seeds = jnp.zeros((K, width), jnp.int32)
    for k in range(K):
        seeds = jnp.where(index == k, seed_ref[k], seeds)
    x_ref[...] = test_matrix(seeds, jnp.broadcast_to(sku_ref[...], (K, width)), width * C)

    def turn(i):
        here = slice((i % SUB) * span, (i % SUB + 1) * span)
        slab_t[i // SUB, :, here] = slab[i * span : (i + 1) * span, :].T

    BULK, GRAM, OWN_GRAM, BLOCK, LAST_GRAM = range(5)

    def remote(kind, src, dst, recv, row, col):
        return pltpu.make_async_remote_copy(
            src_ref=src, dst_ref=dst, send_sem=send_sem.at[kind], recv_sem=recv,
            device_id={"row": row, "col": col}, device_id_type=MESH,
        )

    def sent(kind, ref):
        remote(kind, ref, ref, send_sem.at[kind], me_r, partner).wait_send()

    def sent_rows(kind, values, itemsize):
        sent(kind, slab.at[pl.ds(0, values * itemsize // (2 * width)), :])

    def position(c):
        half = c // Y
        same = 1 - (half + core - 2 * half * core)
        return lax.rem(c, Y) + Y * same

    def swap(it, slot):
        there = (slot + Y) % C
        return remote(BULK, part.at[it, slot], half_recv.at[it, there], a_recv_sem.at[it, there], me_r, partner)

    def swapped(it, slot):
        return remote(BULK, part.at[it, slot], half_recv.at[it, slot], a_recv_sem.at[it, slot], me_r, partner)

    def cross(it, q, k):
        y = lax.rem(me_y + k, Y)
        return remote(
            BULK, y_send.at[it, q], y_sum.at[it, q, me_y], y_recv_sem.at[it, q, k - 1], me_r, y * 2 + other
        )

    def crossed(it, q, k):
        y = lax.rem(me_y + (Y - k), Y)
        return remote(BULK, y_send.at[it, q], y_sum.at[it, q, y], y_recv_sem.at[it, q, k - 1], me_r, partner)

    def square(value):
        return lax.dot_general(
            value, value, (((1,), (1,)), ((), ())), precision=HIGHEST, preferred_element_type=jnp.float32
        )

    def gram_copy(it, h, c):
        slot = lax.rem(me_r * 2 + core - (base + h) * 2 - c - 1 + 4 * R, 2 * R)
        return remote(
            OWN_GRAM if c is core else GRAM, gsend.at[it], grecv.at[it, slot], g_recv_sem.at[it],
            base + h, me_y * 2 + c,
        )

    def z_copy(it, w, h):
        return remote(BULK, zpart.at[it, w, h], zrecv.at[it, w, me_r], z_recv_sem.at[it, w], base + h, partner)

    def back_copy(it, w, row, h):
        cols = pl.ds(pl.multiple_of(h * bw, bw), bw)
        return remote(BLOCK, block_ref.at[it, w], back.at[it, w, :, cols], b_recv_sem.at[it, w], row, partner)

    def landed(ref, sem):
        remote(BULK, ref, ref, sem, me_r, partner).wait_recv()

    def gathered(it):
        def product(w, slot):
            rows = slice(w * wave, (w + 1) * wave)
            return jnp.dot(back[it, w], slab_t[slot, rows, :], preferred_element_type=jnp.float32)

        for w in range(W):
            landed(back.at[it, w], b_recv_sem.at[it, w])
            if w < W - 1:
                for slot in range(C):
                    value = product(w, slot)
                    acc[slot] = value if w == 0 else acc[slot] + value
        if W == 1:
            return lambda slot: product(0, slot)
        return lambda slot: acc[slot] + product(W - 1, slot)

    for it in range(ITERS):
        def hand_over(q):
            swapped(it, Y + q).wait_recv()
            y_send[it, q] = part[it, Y + q] + half_recv[it, Y + q]
            for k in range(1, Y):
                cross(it, q, k).start()

        if it == 0:
            for i in range(n_load):
                k, sub = i // SUB, i % SUB
                here = slice(sub * span, (sub + 1) * span)
                load(i).wait()
                if i + DEPTH < n_load:
                    load(i + DEPTH).start()
                part[it, k, :, here] = lax.dot_general(
                    x_ref[...], slab[i * span : (i + 1) * span, :], (((1,), (1,)), ((), ())), preferred_element_type=jnp.float32
                )
                if i == Y * SUB - 1:
                    pl.semaphore_wait(barrier, R * C - 1)
                    for slot in range(Y):
                        swap(it, slot).start()
                if k >= Y and sub == SUB - 1:
                    swap(it, k).start()
                    hand_over(k - Y)
            for i in TASKS[0]:
                turn(i)
        else:
            last = gathered(it - 1)
            for slot in range(C):
                part[it, slot] = last(slot)
                swap(it, slot).start()
            for q in range(Y):
                hand_over(q)
        for q in range(Y):
            swapped(it, q).wait_recv()
            y_sum[it, q, me_y] = part[it, q] + half_recv[it, q]

        gram = None
        for slot in range(C):
            if slot < Y:
                for k in range(1, Y):
                    crossed(it, slot, k).wait_recv()
                value = y_sum[it, slot, 0]
                for y in range(1, Y):
                    value = value + y_sum[it, slot, y]
                if it > 0:
                    value = value * inv_root
                s_ref[it, slot] = value
                remote(
                    BULK, s_ref.at[it, slot], s_ref.at[it, Y + slot], s_recv_sem.at[it, slot], me_r, partner
                ).start()
                gram = square(value) if slot == 0 else gram + square(value)
                if slot == Y - 1:
                    gsend[it] = gram
                    for k in range(H):
                        h = far(k)
                        gram_copy(it, h, other).start()

                        @pl.when(me_r != base + h)
                        def _():
                            gram_copy(it, h, core).start()

                    grecv[it, 2 * R - 1] = gram
            else:
                landed(s_ref.at[it, slot], s_recv_sem.at[it, slot - Y])
                value = s_ref[it, slot]
            high = value.astype(jnp.bfloat16)
            low = (value - high.astype(jnp.float32)).astype(jnp.bfloat16)
            lhs[:K, :] = high
            lhs[K:, :] = low
            if slot < C - 1:
                product = jnp.dot(lhs[...], slab[slot * piece : (slot + 1) * piece, :], preferred_element_type=jnp.float32)
                product = product[:K] + product[K:]
                zacc[...] = product if slot == 0 else zacc[...] + product
        for w in range(W):
            cols = slice(w * wave, (w + 1) * wave)
            product = jnp.dot(lhs[...], slab[(C - 1) * piece :, cols], preferred_element_type=jnp.float32)
            product = zacc[:, cols] + product[:K] + product[K:]
            for h in range(H):
                zpart[it, w, h] = product[:, h * bw : (h + 1) * bw]
            for k in range(H):
                z_copy(it, w, far(k)).start()

        if it == 0:
            for i in TASKS[1]:
                turn(i)

        @pl.when(is_owner)
        def _():
            landed(grecv.at[it, pl.ds(0, 2 * R - 1)], g_recv_sem.at[it])
            total = grecv[it, 0]
            for r in range(1, 2 * R):
                total = total + grecv[it, r]
            _, inverse = factorize(total)
            own = me_r - base
            for w in range(W):
                if it == 0 and w == W - 1:
                    for i in TASKS[2]:
                        turn(i)
                landed(zrecv.at[it, w], z_recv_sem.at[it, w])
                total = zrecv[it, w, 0]
                for r in range(1, R):
                    total = total + zrecv[it, w, r]
                block_ref[it, w] = jnp.dot(
                    inverse, total, precision=HIGHEST, preferred_element_type=jnp.float32
                ).astype(jnp.bfloat16)
                for k in range(R):
                    back_copy(it, w, far_row(k), own).start()

        if it == 0:
            @pl.when(jnp.logical_not(is_owner))
            def _():
                for i in TASKS[2]:
                    turn(i)

            for i in TASKS[3]:
                turn(i)

    last = gathered(ITERS - 1)

    def to_partner(k):
        y = lax.rem(me_y + k, Y)
        return remote(BULK, fin_part.at[k], fin_recv.at[k], f_recv_sem.at[k], me_r, partner), y

    for k in list(range(1, Y)) + [0]:
        copy, y = to_partner(k)
        fin_part[k] = last(position(y * 2 + (core if k else other)))
        copy.start()
    for k in list(range(1, Y)) + [0]:
        y = lax.rem(me_y + k, Y)
        fin_send[k] = last(position(y * 2 + (other if k else core)))
    outer = []
    for k in range(1, Y):
        copy, y = to_partner(k)
        copy.wait_recv()
        fin_send[k] = fin_send[k] + fin_recv[k]
        copy = remote(BULK, fin_send.at[k], fin_y.at[k], fy_recv_sem.at[k - 1], me_r, y * 2 + other)
        copy.start()
        outer.append(copy)
    to_partner(0)[0].wait_recv()
    own = fin_send[0] + fin_recv[0]
    for k, copy in enumerate(outer):
        copy.wait_recv()
        own = own + fin_y[k + 1]
    own = own * inv_root
    fsend[...] = square(own)

    n = R * C

    def spread(k):
        pltpu.make_async_remote_copy(
            src_ref=fsend, dst_ref=frecv.at[n - 1 - k], send_sem=send_sem.at[LAST_GRAM],
            recv_sem=c_recv_sem.at[0], device_id=peer(k), device_id_type=MESH,
        ).start()

    repeat(1, n, spread)
    frecv[n - 1] = fsend[...]

    moved = ITERS * (C + Y * (Y - 1) + Y) * K * piece + ITERS * K * width + (2 * Y - 1) * K * piece
    sent_rows(BULK, moved, 4)
    sent(GRAM, frecv.at[pl.ds(0, ITERS * H)])

    @pl.when(is_owner)
    def _():
        sent(OWN_GRAM, frecv.at[pl.ds(0, ITERS * (H - 1))])
        sent_rows(BLOCK, ITERS * W * R * K * bw, 2)

    @pl.when(jnp.logical_not(is_owner))
    def _():
        sent(OWN_GRAM, frecv.at[pl.ds(0, ITERS * H)])

    landed(frecv.at[pl.ds(0, n - 1)], c_recv_sem.at[0])
    def held(d):
        return frecv[lax.rem(d - me - 1 + n, n)]

    parts = [held(d) for d in range(8)]
    for d in range(8, n):
        parts[d % 8] = parts[d % 8] + held(d)
    while len(parts) > 1:
        parts = [a + b for a, b in zip(parts[::2], parts[1::2])]
    upper, inverse = factorize(parts[0])
    ortho = jnp.dot(inverse, own, precision=HIGHEST, preferred_element_type=jnp.float32)
    basis_ref[...] = ortho * scale
    factor_ref[...] = upper / scale
    sent(LAST_GRAM, frecv.at[pl.ds(0, n - 1)])


def body(affinity, seed_values, sku_ids):
    R, C = lax.axis_size("row"), lax.axis_size("col")
    K = seed_values.shape[0]
    rows, width = affinity.shape
    piece, Y = rows // C, C // 2
    H = min(R // 2, width // LANES)
    W = 2 if width % (2 * H * LANES) == 0 else 1
    base, wave, bw = (R - H) // 2, width // W, width // W // H
    dims = (R, C, K, piece, width, base, H, W, 1.0 / math.sqrt(width * C), math.sqrt(rows * R))
    f32, bf16 = jnp.float32, jnp.bfloat16
    dma = pltpu.SemaphoreType.DMA
    vmem = pl.BlockSpec(memory_space=pltpu.VMEM)
    return pl.pallas_call(
        functools.partial(kernel, dims),
        out_shape=(
            pltpu.VMEM((K, piece), f32),
            pltpu.VMEM((K, K), f32),
        ),
        in_specs=[pl.BlockSpec(memory_space=pl.ANY)] * 3,
        out_specs=(vmem, vmem),
        scratch_shapes=[
            pltpu.VMEM((rows, width), bf16),
            pltpu.VMEM((C, width, piece), bf16),
            pltpu.SMEM((K,), jnp.int32),
            pltpu.VMEM((1, width), jnp.int32),
            pltpu.VMEM((K, width), bf16),
            pltpu.VMEM((C, K, piece), f32),
            pltpu.VMEM((ITERS, C, K, piece), f32),
            pltpu.VMEM((ITERS, C, K, piece), f32),
            pltpu.VMEM((ITERS, Y, K, piece), f32),
            pltpu.VMEM((ITERS, Y, Y, K, piece), f32),
            pltpu.VMEM((Y, K, piece), f32),
            pltpu.VMEM((Y, K, piece), f32),
            pltpu.VMEM((Y, K, piece), f32),
            pltpu.VMEM((Y, K, piece), f32),
            pltpu.VMEM((ITERS, C, K, piece), f32),
            pltpu.VMEM((2 * K, piece), bf16),
            pltpu.VMEM((K, width), f32),
            pltpu.VMEM((ITERS, W, H, K, bw), f32),
            pltpu.VMEM((ITERS, W, R, K, bw), f32),
            pltpu.VMEM((ITERS, W, K, bw), bf16),
            pltpu.VMEM((ITERS, W, K, wave), bf16),
            pltpu.VMEM((ITERS, K, K), f32),
            pltpu.VMEM((ITERS, 2 * R, K, K), f32),
            pltpu.VMEM((K, K), f32),
            pltpu.VMEM((R * C, K, K), f32),
            dma((DEPTH + 2,)),
            dma((5,)),
            dma((ITERS, C)),
            dma((ITERS, Y, Y - 1)),
            dma((Y,)),
            dma((Y - 1,)),
            dma((ITERS, Y)),
            dma((ITERS, W)),
            dma((ITERS, W)),
            dma((ITERS,)),
            dma((1,)),
        ],
        compiler_params=pltpu.CompilerParams(
            collective_id=0, has_side_effects=True, vmem_limit_bytes=60 * 1024 * 1024
        ),
    )(affinity, seed_values, sku_ids[None, :])


def solution(mesh):
    placed = (P("row", "col"), P(), P("col"))
    return jax.shard_map(
        body, mesh=mesh, in_specs=placed, out_specs=(P(None, ("row", "col")), P()), check_vma=False
    )
```

```python
import functools
import math

import jax
import jax.numpy as jnp
from jax import lax
from jax.experimental import pallas as pl
from jax.experimental.pallas import tpu as pltpu
from jax.sharding import PartitionSpec as P

ITERS = 2
SUB = 2
CUT = 2
DEPTH = 4
LANES = 128
TASKS = ((0, 1), (2, 3, 4), (5,), (6, 7))
HIGHEST = lax.Precision.HIGHEST
MESH = pl.DeviceIdType.MESH

mix_first = -2048144789
mix_second = -1028477387
golden = -1640531535
salt_value = 1540483477


def shifted(value, amount):
    return lax.shift_right_logical(value, jnp.full(value.shape, amount, jnp.int32))


def scramble(value):
    value = jnp.bitwise_xor(value, shifted(value, 16))
    value = value * jnp.int32(mix_first)
    value = jnp.bitwise_xor(value, shifted(value, 13))
    value = value * jnp.int32(mix_second)
    return jnp.bitwise_xor(value, shifted(value, 16))


def test_matrix(seeds, skus, total_columns):
    first = scramble(jnp.bitwise_xor(seeds, skus * jnp.int32(golden)))
    second = scramble(jnp.bitwise_xor(first, jnp.int32(salt_value)))
    uniform_a = (shifted(first, 9) + 1).astype(jnp.float32) / 8388608.0
    uniform_b = (shifted(second, 9) + 1).astype(jnp.float32) / 8388608.0
    gauss = jnp.sqrt(-2.0 * jnp.log(uniform_a)) * jnp.cos(6.283185307179586 * uniform_b)
    return (gauss / math.sqrt(total_columns)).astype(jnp.bfloat16)


def refined_rsqrt(value):
    root = lax.rsqrt(value)
    return root * (1.5 - 0.5 * (value * root) * root)


def factorize(gram, right):
    count = gram.shape[0]
    shape = (count, LANES)
    rows = lax.broadcasted_iota(jnp.int32, shape, 0)
    cols = lax.broadcasted_iota(jnp.int32, shape, 1)
    top = jnp.max(jnp.max(gram, axis=1, keepdims=True), axis=0, keepdims=True)
    scale = refined_rsqrt(top)
    left = jnp.concatenate([gram * (1.0 / top), jnp.zeros((count, LANES - count), jnp.float32)], axis=1)
    arrays = [left] + list(right)
    results = [jnp.zeros(shape, jnp.float32) for _ in arrays]
    for j in range(0, count, 2):
        first = jnp.broadcast_to(arrays[0][:, j : j + 1], shape)
        second = jnp.broadcast_to(arrays[0][:, j + 1 : j + 2], shape)
        a, b, c = first[j : j + 1], first[j + 1 : j + 2], second[j + 1 : j + 2]
        det = a * c - b * b
        inv = 1.0 / det
        below = rows > j + 1
        one = jnp.where(below, first * c - second * b, 0.0) * inv
        two = jnp.where(below, second * a - first * b, 0.0) * inv
        root = refined_rsqrt(a)
        next_root = refined_rsqrt(det) * (a * root)
        ratio = b * root * root
        for i, array in enumerate(arrays):
            head, tail = array[j : j + 1], array[j + 1 : j + 2]
            results[i] = jnp.where(
                rows == j, head * root, jnp.where(rows == j + 1, (tail - ratio * head) * next_root, results[i])
            )
            arrays[i] = array - (one * head + two * tail)
    upper = jnp.where(rows <= cols, results[0], 0.0) * (top * scale)
    return upper[:, :count], [array * scale for array in results[1:]]


def repeat(start, stop, step):
    if stop - start <= 64:
        for k in range(start, stop):
            step(k)
    else:
        lax.fori_loop(start, stop, lambda k, _: (step(k), 0)[1], 0)


def kernel(
    dims,
    slab_hbm, seed_hbm, sku_hbm,
    basis_ref, factor_ref,
    slab, slab_t, seed_ref, sku_ref, x_ref, acc, part, half_recv, y_send, y_sum,
    fin_part, fin_recv, fin_send, fin_y, s_ref, lhs, zacc, zpart, zrecv, block_ref, back,
    gsend, grecv, fsend, frecv,
    load_sem, send_sem, a_recv_sem, y_recv_sem, f_recv_sem, fy_recv_sem, s_recv_sem, z_recv_sem, b_recv_sem,
    g_recv_sem, c_recv_sem,
):
    R, C, K, piece, width, base, H, W, inv_root, scale = dims
    wave = width // W
    bw = wave // H
    me_r = lax.axis_index("row")
    me_c = lax.axis_index("col")
    me = me_r * C + me_c

    Y = C // 2
    core, me_y = lax.rem(me_c, 2), me_c // 2
    other = 1 - core
    partner = me_y * 2 + other

    flip = me_r // (R // 2)
    is_owner = jnp.logical_and(me_r >= base, me_r < base + H)

    def far(k):
        return (H - 1 - k) + flip * (2 * k - H + 1)

    def far_row(k):
        return (R - 1 - k) + flip * (2 * k - R + 1)

    span, unit, units = piece // SUB, piece // CUT, C * CUT
    n_load = C * SUB

    def load(i):
        k = i // SUB
        start = ((other * Y + k) if k < Y else (core * Y + k - Y)) * piece + (i % SUB) * span
        return pltpu.make_async_copy(
            slab_hbm.at[pl.ds(pl.multiple_of(start, span), span), :],
            slab.at[pl.ds(i * span, span), :],
            load_sem.at[i % DEPTH],
        )

    seed_copy = pltpu.make_async_copy(seed_hbm, seed_ref, load_sem.at[DEPTH])
    sku_copy = pltpu.make_async_copy(sku_hbm, sku_ref, load_sem.at[DEPTH + 1])
    seed_copy.start()
    sku_copy.start()
    for i in range(min(DEPTH, n_load)):
        load(i).start()

    def peer(k):
        index = lax.rem(me + k, R * C)
        return {"row": index // C, "col": lax.rem(index, C)}

    barrier = pltpu.get_barrier_semaphore()

    def greet(k):
        pl.semaphore_signal(barrier, inc=1, device_id=peer(k), device_id_type=MESH)

    repeat(1, R * C, greet)

    seed_copy.wait()
    sku_copy.wait()
    index = lax.broadcasted_iota(jnp.int32, (K, width), 0)
    seeds = jnp.zeros((K, width), jnp.int32)
    for k in range(K):
        seeds = jnp.where(index == k, seed_ref[k], seeds)
    x_ref[...] = test_matrix(seeds, jnp.broadcast_to(sku_ref[...], (K, width)), width * C)

    def turn(i):
        here = slice((i % SUB) * span, (i % SUB + 1) * span)
        slab_t[i // SUB, :, here] = slab[i * span : (i + 1) * span, :].T

    BULK, GRAM, OWN_GRAM, BLOCK, LAST_GRAM = range(5)

    def remote(kind, src, dst, recv, row, col):
        return pltpu.make_async_remote_copy(
            src_ref=src, dst_ref=dst, send_sem=send_sem.at[kind], recv_sem=recv,
            device_id={"row": row, "col": col}, device_id_type=MESH,
        )

    def sent(kind, ref):
        remote(kind, ref, ref, send_sem.at[kind], me_r, partner).wait_send()

    def sent_rows(kind, values, itemsize):
        sent(kind, slab.at[pl.ds(0, values * itemsize // (2 * width)), :])

    def position(c):
        half = c // Y
        same = 1 - (half + core - 2 * half * core)
        return lax.rem(c, Y) + Y * same

    def swap(it, slot):
        there = (slot + Y) % C
        return remote(BULK, part.at[it, slot], half_recv.at[it, there], a_recv_sem.at[it, there], me_r, partner)

    def swapped(it, slot):
        return remote(BULK, part.at[it, slot], half_recv.at[it, slot], a_recv_sem.at[it, slot], me_r, partner)

    def cross(it, q, k):
        y = lax.rem(me_y + k, Y)
        return remote(
            BULK, y_send.at[it, q], y_sum.at[it, q, me_y], y_recv_sem.at[it, q, k - 1], me_r, y * 2 + other
        )

    def crossed(it, q, k):
        y = lax.rem(me_y + (Y - k), Y)
        return remote(BULK, y_send.at[it, q], y_sum.at[it, q, y], y_recv_sem.at[it, q, k - 1], me_r, partner)

    def square(value):
        return lax.dot_general(
            value, value, (((1,), (1,)), ((), ())), precision=HIGHEST, preferred_element_type=jnp.float32
        )

    def gram_copy(it, h, c):
        slot = lax.rem(me_r * 2 + core - (base + h) * 2 - c - 1 + 4 * R, 2 * R)
        return remote(
            OWN_GRAM if c is core else GRAM, gsend.at[it], grecv.at[it, slot], g_recv_sem.at[it],
            base + h, me_y * 2 + c,
        )

    def z_copy(it, w, h):
        return remote(BULK, zpart.at[it, w, h], zrecv.at[it, w, me_r], z_recv_sem.at[it, w], base + h, partner)

    def back_copy(it, w, row, h):
        cols = pl.ds(pl.multiple_of(h * bw, bw), bw)
        return remote(BLOCK, block_ref.at[it, w], back.at[it, w, :, cols], b_recv_sem.at[it, w], row, partner)

    def landed(ref, sem):
        remote(BULK, ref, ref, sem, me_r, partner).wait_recv()

    def gathered(it):
        def product(w, slot):
            rows = slice(w * wave, (w + 1) * wave)
            return jnp.dot(back[it, w], slab_t[slot, rows, :], preferred_element_type=jnp.float32)

        for w in range(W):
            landed(back.at[it, w], b_recv_sem.at[it, w])
            if w < W - 1:
                for slot in range(C):
                    value = product(w, slot)
                    acc[slot] = value if w == 0 else acc[slot] + value
        if W == 1:
            return lambda slot: product(0, slot)
        return lambda slot: acc[slot] + product(W - 1, slot)

    for it in range(ITERS):
        def hand_over(q):
            swapped(it, Y + q).wait_recv()
            for u in range(CUT):
                here = slice(u * unit, (u + 1) * unit)
                y_send[it, q * CUT + u] = part[it, Y + q, :, here] + half_recv[it, Y + q, :, here]
                for k in range(1, Y):
                    cross(it, q * CUT + u, k).start()

        if it == 0:
            for i in range(n_load):
                k, sub = i // SUB, i % SUB
                here = slice(sub * span, (sub + 1) * span)
                load(i).wait()
                if i + DEPTH < n_load:
                    load(i + DEPTH).start()
                part[it, k, :, here] = lax.dot_general(
                    x_ref[...], slab[i * span : (i + 1) * span, :], (((1,), (1,)), ((), ())), preferred_element_type=jnp.float32
                )
                if i == Y * SUB - 1:
                    pl.semaphore_wait(barrier, R * C - 1)
                    for slot in range(Y):
                        swap(it, slot).start()
                if k >= Y and sub == SUB - 1:
                    swap(it, k).start()
                    hand_over(k - Y)
            for i in TASKS[0]:
                turn(i)
        else:
            last = gathered(it - 1)
            for q in range(Y):
                for slot in (q, Y + q):
                    part[it, slot] = last(slot)
                    swap(it, slot).start()
                    if q > 0 and slot == q:
                        hand_over(q - 1)
            hand_over(Y - 1)
        for q in range(Y):
            swapped(it, q).wait_recv()
            for u in range(CUT):
                here = slice(u * unit, (u + 1) * unit)
                y_sum[it, q * CUT + u, me_y] = part[it, q, :, here] + half_recv[it, q, :, here]

        gram = None
        for n in range(units):
            if n < units // 2:
                for k in range(1, Y):
                    crossed(it, n, k).wait_recv()
                value = y_sum[it, n, 0]
                for y in range(1, Y):
                    value = value + y_sum[it, n, y]
                if it > 0:
                    value = value * inv_root
                s_ref[it, n] = value
                remote(
                    BULK, s_ref.at[it, n], s_ref.at[it, units // 2 + n], s_recv_sem.at[it, n], me_r, partner
                ).start()
                gram = square(value) if n == 0 else gram + square(value)
                if n == units // 2 - 1:
                    gsend[it] = gram
                    for k in range(H):
                        h = far(k)
                        gram_copy(it, h, other).start()

                        @pl.when(me_r != base + h)
                        def _():
                            gram_copy(it, h, core).start()

                    grecv[it, 2 * R - 1] = gram
            else:
                landed(s_ref.at[it, n], s_recv_sem.at[it, n - units // 2])
                value = s_ref[it, n]
            high = value.astype(jnp.bfloat16)
            low = (value - high.astype(jnp.float32)).astype(jnp.bfloat16)
            lhs[n % 2, :K, :] = high
            lhs[n % 2, K:, :] = low
            if n < units - 1:
                product = jnp.dot(
                    lhs[n % 2], slab[n * unit : (n + 1) * unit, :], preferred_element_type=jnp.float32
                )
                product = product[:K] + product[K:]
                zacc[...] = product if n == 0 else zacc[...] + product
        for w in range(W):
            cols = slice(w * wave, (w + 1) * wave)
            product = jnp.dot(
                lhs[(units - 1) % 2], slab[(units - 1) * unit :, cols], preferred_element_type=jnp.float32
            )
            product = zacc[:, cols] + product[:K] + product[K:]
            for h in range(H):
                zpart[it, w, h] = product[:, h * bw : (h + 1) * bw]
            for k in range(H):
                z_copy(it, w, far(k)).start()

        if it == 0:
            for i in TASKS[1]:
                turn(i)

        @pl.when(is_owner)
        def _():
            landed(grecv.at[it, pl.ds(0, 2 * R - 1)], g_recv_sem.at[it])
            total = grecv[it, 0]
            for r in range(1, 2 * R):
                total = total + grecv[it, r]
            identity = lax.broadcasted_iota(jnp.int32, (K, LANES), 0) == lax.broadcasted_iota(jnp.int32, (K, LANES), 1)
            inverse = factorize(total, [identity.astype(jnp.float32)])[1][0][:, :K]
            own = me_r - base
            for w in range(W):
                if it == 0 and w == W - 1:
                    for i in TASKS[2]:
                        turn(i)
                landed(zrecv.at[it, w], z_recv_sem.at[it, w])
                total = zrecv[it, w, 0]
                for r in range(1, R):
                    total = total + zrecv[it, w, r]
                block_ref[it, w] = jnp.dot(
                    inverse, total, precision=HIGHEST, preferred_element_type=jnp.float32
                ).astype(jnp.bfloat16)
                for k in range(R):
                    back_copy(it, w, far_row(k), own).start()

        if it == 0:
            @pl.when(jnp.logical_not(is_owner))
            def _():
                for i in TASKS[2]:
                    turn(i)

            for i in TASKS[3]:
                turn(i)

    last = gathered(ITERS - 1)

    def to_partner(k):
        y = lax.rem(me_y + k, Y)
        return remote(BULK, fin_part.at[k], fin_recv.at[k], f_recv_sem.at[k], me_r, partner), y

    for k in list(range(1, Y)) + [0]:
        copy, y = to_partner(k)
        fin_part[k] = last(position(y * 2 + (core if k else other)))
        copy.start()
    for k in list(range(1, Y)) + [0]:
        y = lax.rem(me_y + k, Y)
        fin_send[k] = last(position(y * 2 + (other if k else core)))
    outer = []
    for k in range(1, Y):
        copy, y = to_partner(k)
        copy.wait_recv()
        fin_send[k] = fin_send[k] + fin_recv[k]
        copy = remote(BULK, fin_send.at[k], fin_y.at[k], fy_recv_sem.at[k - 1], me_r, y * 2 + other)
        copy.start()
        outer.append(copy)
    to_partner(0)[0].wait_recv()
    own = fin_send[0] + fin_recv[0]
    for k, copy in enumerate(outer):
        copy.wait_recv()
        own = own + fin_y[k + 1]
    own = own * inv_root
    fsend[...] = square(own)

    n = R * C

    def spread(k):
        pltpu.make_async_remote_copy(
            src_ref=fsend, dst_ref=frecv.at[n - 1 - k], send_sem=send_sem.at[LAST_GRAM],
            recv_sem=c_recv_sem.at[0], device_id=peer(k), device_id_type=MESH,
        ).start()

    repeat(1, n, spread)
    frecv[n - 1] = fsend[...]

    moved = ITERS * (C + Y * (Y - 1) + Y) * K * piece + ITERS * K * width + (2 * Y - 1) * K * piece
    sent_rows(BULK, moved, 4)
    sent(GRAM, frecv.at[pl.ds(0, ITERS * H)])

    @pl.when(is_owner)
    def _():
        sent(OWN_GRAM, frecv.at[pl.ds(0, ITERS * (H - 1))])
        sent_rows(BLOCK, ITERS * W * R * K * bw, 2)

    @pl.when(jnp.logical_not(is_owner))
    def _():
        sent(OWN_GRAM, frecv.at[pl.ds(0, ITERS * H)])

    landed(frecv.at[pl.ds(0, n - 1)], c_recv_sem.at[0])
    def held(d):
        return frecv[lax.rem(d - me - 1 + n, n)]

    parts = [held(d) for d in range(8)]
    for d in range(8, n):
        parts[d % 8] = parts[d % 8] + held(d)
    while len(parts) > 1:
        parts = [a + b for a, b in zip(parts[::2], parts[1::2])]
    chunks = [slice(i, i + LANES) for i in range(0, piece, LANES)]
    upper, ortho = factorize(parts[0], [own[:, chunk] for chunk in chunks])
    for chunk, array in zip(chunks, ortho):
        basis_ref[:, chunk] = array * scale
    factor_ref[...] = upper / scale
    sent(LAST_GRAM, frecv.at[pl.ds(0, n - 1)])


def body(affinity, seed_values, sku_ids):
    R, C = lax.axis_size("row"), lax.axis_size("col")
    K = seed_values.shape[0]
    rows, width = affinity.shape
    piece, Y = rows // C, C // 2
    H = min(R // 2, width // LANES)
    W = 4 if width % (4 * H * LANES) == 0 else 1
    base, wave, bw = (R - H) // 2, width // W, width // W // H
    dims = (R, C, K, piece, width, base, H, W, 1.0 / math.sqrt(width * C), math.sqrt(rows * R))
    f32, bf16 = jnp.float32, jnp.bfloat16
    dma = pltpu.SemaphoreType.DMA
    vmem = pl.BlockSpec(memory_space=pltpu.VMEM)
    return pl.pallas_call(
        functools.partial(kernel, dims),
        out_shape=(
            pltpu.VMEM((K, piece), f32),
            pltpu.VMEM((K, K), f32),
        ),
        in_specs=[pl.BlockSpec(memory_space=pl.ANY)] * 3,
        out_specs=(vmem, vmem),
        scratch_shapes=[
            pltpu.VMEM((rows, width), bf16),
            pltpu.VMEM((C, width, piece), bf16),
            pltpu.SMEM((K,), jnp.int32),
            pltpu.VMEM((1, width), jnp.int32),
            pltpu.VMEM((K, width), bf16),
            pltpu.VMEM((C, K, piece), f32),
            pltpu.VMEM((ITERS, C, K, piece), f32),
            pltpu.VMEM((ITERS, C, K, piece), f32),
            pltpu.VMEM((ITERS, Y * CUT, K, piece // CUT), f32),
            pltpu.VMEM((ITERS, Y * CUT, Y, K, piece // CUT), f32),
            pltpu.VMEM((Y, K, piece), f32),
            pltpu.VMEM((Y, K, piece), f32),
            pltpu.VMEM((Y, K, piece), f32),
            pltpu.VMEM((Y, K, piece), f32),
            pltpu.VMEM((ITERS, C * CUT, K, piece // CUT), f32),
            pltpu.VMEM((2, 2 * K, piece // CUT), bf16),
            pltpu.VMEM((K, width), f32),
            pltpu.VMEM((ITERS, W, H, K, bw), f32),
            pltpu.VMEM((ITERS, W, R, K, bw), f32),
            pltpu.VMEM((ITERS, W, K, bw), bf16),
            pltpu.VMEM((ITERS, W, K, wave), bf16),
            pltpu.VMEM((ITERS, K, K), f32),
            pltpu.VMEM((ITERS, 2 * R, K, K), f32),
            pltpu.VMEM((K, K), f32),
            pltpu.VMEM((R * C, K, K), f32),
            dma((DEPTH + 2,)),
            dma((5,)),
            dma((ITERS, C)),
            dma((ITERS, Y * CUT, Y - 1)),
            dma((Y,)),
            dma((Y - 1,)),
            dma((ITERS, Y * CUT)),
            dma((ITERS, W)),
            dma((ITERS, W)),
            dma((ITERS,)),
            dma((1,)),
        ],
        compiler_params=pltpu.CompilerParams(
            collective_id=0, has_side_effects=True, vmem_limit_bytes=60 * 1024 * 1024
        ),
    )(affinity, seed_values, sku_ids[None, :])


def solution(mesh):
    placed = (P("row", "col"), P(), P("col"))
    return jax.shard_map(
        body, mesh=mesh, in_specs=placed, out_specs=(P(None, ("row", "col")), P()), check_vma=False
    )
```

```python
import functools
import math

import jax
import jax.numpy as jnp
from jax import lax
from jax.experimental import pallas as pl
from jax.experimental.pallas import tpu as pltpu
from jax.sharding import PartitionSpec as P

ITERS = 2
SUB = 2
CUT = 2
DEPTH = 4
LANES = 128
TASKS = ((0, 1), (2, 3, 4), (5,), (6, 7))
HIGHEST = lax.Precision.HIGHEST
MESH = pl.DeviceIdType.MESH

mix_first = -2048144789
mix_second = -1028477387
golden = -1640531535
salt_value = 1540483477


def shifted(value, amount):
    return lax.shift_right_logical(value, jnp.full(value.shape, amount, jnp.int32))


def scramble(value):
    value = jnp.bitwise_xor(value, shifted(value, 16))
    value = value * jnp.int32(mix_first)
    value = jnp.bitwise_xor(value, shifted(value, 13))
    value = value * jnp.int32(mix_second)
    return jnp.bitwise_xor(value, shifted(value, 16))


def test_matrix(seeds, skus, total_columns):
    first = scramble(jnp.bitwise_xor(seeds, skus * jnp.int32(golden)))
    second = scramble(jnp.bitwise_xor(first, jnp.int32(salt_value)))
    uniform_a = (shifted(first, 9) + 1).astype(jnp.float32) / 8388608.0
    uniform_b = (shifted(second, 9) + 1).astype(jnp.float32) / 8388608.0
    gauss = jnp.sqrt(-2.0 * jnp.log(uniform_a)) * jnp.cos(6.283185307179586 * uniform_b)
    return (gauss / math.sqrt(total_columns)).astype(jnp.bfloat16)


def refined_rsqrt(value):
    root = lax.rsqrt(value)
    return root * (1.5 - 0.5 * (value * root) * root)


def factorize(gram, right):
    count = gram.shape[0]
    shape = (count, LANES)
    rows = lax.broadcasted_iota(jnp.int32, shape, 0)
    cols = lax.broadcasted_iota(jnp.int32, shape, 1)
    top = jnp.max(jnp.max(gram, axis=1, keepdims=True), axis=0, keepdims=True)
    scale = refined_rsqrt(top)
    left = jnp.concatenate([gram * (1.0 / top), jnp.zeros((count, LANES - count), jnp.float32)], axis=1)
    arrays = [left] + list(right)
    results = [jnp.zeros(shape, jnp.float32) for _ in arrays]
    for j in range(0, count, 2):
        first = jnp.broadcast_to(arrays[0][:, j : j + 1], shape)
        second = jnp.broadcast_to(arrays[0][:, j + 1 : j + 2], shape)
        a, b, c = first[j : j + 1], first[j + 1 : j + 2], second[j + 1 : j + 2]
        det = a * c - b * b
        inv = 1.0 / det
        below = rows > j + 1
        one = jnp.where(below, first * c - second * b, 0.0) * inv
        two = jnp.where(below, second * a - first * b, 0.0) * inv
        root = refined_rsqrt(a)
        next_root = refined_rsqrt(det) * (a * root)
        ratio = b * root * root
        for i, array in enumerate(arrays):
            head, tail = array[j : j + 1], array[j + 1 : j + 2]
            results[i] = jnp.where(
                rows == j, head * root, jnp.where(rows == j + 1, (tail - ratio * head) * next_root, results[i])
            )
            arrays[i] = array - (one * head + two * tail)
    upper = jnp.where(rows <= cols, results[0], 0.0) * (top * scale)
    return upper[:, :count], [array * scale for array in results[1:]]


def repeat(start, stop, step):
    if stop - start <= 64:
        for k in range(start, stop):
            step(k)
    else:
        lax.fori_loop(start, stop, lambda k, _: (step(k), 0)[1], 0)


def kernel(
    dims,
    slab_hbm, seed_hbm, sku_hbm,
    basis_ref, factor_ref,
    slab, slab_t, seed_ref, sku_ref, x_ref, acc, part, half_recv, y_send, y_sum,
    fin_part, fin_recv, fin_send, fin_y, s_ref, lhs, zacc, zpart, zrecv, block_ref, back,
    gsend, grecv, fsend, frecv,
    load_sem, send_sem, a_recv_sem, y_recv_sem, f_recv_sem, fy_recv_sem, s_recv_sem, z_recv_sem, b_recv_sem,
    g_recv_sem, c_recv_sem,
):
    R, C, K, piece, width, base, H, W, inv_root, scale = dims
    wave = width // W
    bw = wave // H
    me_r = lax.axis_index("row")
    me_c = lax.axis_index("col")
    me = me_r * C + me_c

    Y = C // 2
    core, me_y = lax.rem(me_c, 2), me_c // 2
    other = 1 - core
    partner = me_y * 2 + other

    flip = me_r // (R // 2)
    is_owner = jnp.logical_and(me_r >= base, me_r < base + H)

    def far(k):
        return (H - 1 - k) + flip * (2 * k - H + 1)

    def far_row(k):
        return (R - 1 - k) + flip * (2 * k - R + 1)

    span, unit, units = piece // SUB, piece // CUT, C * CUT
    n_load = C * SUB

    def load(i):
        k = i // SUB
        start = ((other * Y + k) if k < Y else (core * Y + k - Y)) * piece + (i % SUB) * span
        return pltpu.make_async_copy(
            slab_hbm.at[pl.ds(pl.multiple_of(start, span), span), :],
            slab.at[pl.ds(i * span, span), :],
            load_sem.at[i % DEPTH],
        )

    seed_copy = pltpu.make_async_copy(seed_hbm, seed_ref, load_sem.at[DEPTH])
    sku_copy = pltpu.make_async_copy(sku_hbm, sku_ref, load_sem.at[DEPTH + 1])
    seed_copy.start()
    sku_copy.start()
    for i in range(min(DEPTH, n_load)):
        load(i).start()

    def peer(k):
        index = lax.rem(me + k, R * C)
        return {"row": index // C, "col": lax.rem(index, C)}

    barrier = pltpu.get_barrier_semaphore()

    def greet(k):
        pl.semaphore_signal(barrier, inc=1, device_id=peer(k), device_id_type=MESH)

    repeat(1, R * C, greet)

    seed_copy.wait()
    sku_copy.wait()
    index = lax.broadcasted_iota(jnp.int32, (K, width), 0)
    seeds = jnp.zeros((K, width), jnp.int32)
    for k in range(K):
        seeds = jnp.where(index == k, seed_ref[k], seeds)
    x_ref[...] = test_matrix(seeds, jnp.broadcast_to(sku_ref[...], (K, width)), width * C)

    def turn(i):
        here = slice((i % SUB) * span, (i % SUB + 1) * span)
        slab_t[i // SUB, :, here] = slab[i * span : (i + 1) * span, :].T

    BULK, GRAM, OWN_GRAM, BLOCK, LAST_GRAM = range(5)

    def remote(kind, src, dst, recv, row, col):
        return pltpu.make_async_remote_copy(
            src_ref=src, dst_ref=dst, send_sem=send_sem.at[kind], recv_sem=recv,
            device_id={"row": row, "col": col}, device_id_type=MESH,
        )

    def sent(kind, ref):
        remote(kind, ref, ref, send_sem.at[kind], me_r, partner).wait_send()

    def sent_rows(kind, values, itemsize):
        sent(kind, slab.at[pl.ds(0, values * itemsize // (2 * width)), :])

    def position(c):
        half = c // Y
        same = 1 - (half + core - 2 * half * core)
        return lax.rem(c, Y) + Y * same

    def swap(it, slot):
        there = (slot + Y) % C
        return remote(BULK, part.at[it, slot], half_recv.at[it, there], a_recv_sem.at[it, there], me_r, partner)

    def swapped(it, slot):
        return remote(BULK, part.at[it, slot], half_recv.at[it, slot], a_recv_sem.at[it, slot], me_r, partner)

    def cross(it, q, k):
        y = lax.rem(me_y + k, Y)
        return remote(
            BULK, y_send.at[it, q], y_sum.at[it, q, me_y], y_recv_sem.at[it, q, k - 1], me_r, y * 2 + other
        )

    def crossed(it, q, k):
        y = lax.rem(me_y + (Y - k), Y)
        return remote(BULK, y_send.at[it, q], y_sum.at[it, q, y], y_recv_sem.at[it, q, k - 1], me_r, partner)

    def square(value):
        return lax.dot_general(
            value, value, (((1,), (1,)), ((), ())), precision=HIGHEST, preferred_element_type=jnp.float32
        )

    def gram_copy(it, h, c):
        slot = lax.rem(me_r * 2 + core - (base + h) * 2 - c - 1 + 4 * R, 2 * R)
        return remote(
            OWN_GRAM if c is core else GRAM, gsend.at[it], grecv.at[it, slot], g_recv_sem.at[it],
            base + h, me_y * 2 + c,
        )

    def z_copy(it, w, h):
        return remote(BULK, zpart.at[it, w, h], zrecv.at[it, w, me_r], z_recv_sem.at[it, w], base + h, partner)

    def back_copy(it, w, row, h):
        cols = pl.ds(pl.multiple_of(h * bw, bw), bw)
        return remote(BLOCK, block_ref.at[it, w], back.at[it, w, :, cols], b_recv_sem.at[it, w], row, partner)

    def landed(ref, sem):
        remote(BULK, ref, ref, sem, me_r, partner).wait_recv()

    def gathered(it):
        def product(w, slot):
            rows = slice(w * wave, (w + 1) * wave)
            return jnp.dot(back[it, w], slab_t[slot, rows, :], preferred_element_type=jnp.float32)

        for w in range(W):
            landed(back.at[it, w], b_recv_sem.at[it, w])
            if w < W - 1:
                for slot in range(C):
                    value = product(w, slot)
                    acc[slot] = value if w == 0 else acc[slot] + value
        if W == 1:
            return lambda slot: product(0, slot)
        return lambda slot: acc[slot] + product(W - 1, slot)

    for it in range(ITERS):
        def hand_over(q):
            swapped(it, Y + q).wait_recv()
            for u in range(CUT):
                here = slice(u * unit, (u + 1) * unit)
                y_send[it, q * CUT + u] = part[it, Y + q, :, here] + half_recv[it, Y + q, :, here]
                for k in range(1, Y):
                    cross(it, q * CUT + u, k).start()

        if it == 0:
            for i in range(n_load):
                k, sub = i // SUB, i % SUB
                here = slice(sub * span, (sub + 1) * span)
                load(i).wait()
                if i + DEPTH < n_load:
                    load(i + DEPTH).start()
                part[it, k, :, here] = lax.dot_general(
                    x_ref[...], slab[i * span : (i + 1) * span, :], (((1,), (1,)), ((), ())), preferred_element_type=jnp.float32
                )
                if i == Y * SUB - 1:
                    pl.semaphore_wait(barrier, R * C - 1)
                    for slot in range(Y):
                        swap(it, slot).start()
                if k >= Y and sub == SUB - 1:
                    swap(it, k).start()
                    hand_over(k - Y)
            for i in TASKS[0]:
                turn(i)
        else:
            last = gathered(it - 1)
            for q in range(Y):
                for slot in (q, Y + q):
                    part[it, slot] = last(slot)
                    swap(it, slot).start()
                    if q > 0 and slot == q:
                        hand_over(q - 1)
            hand_over(Y - 1)
        for q in range(Y):
            swapped(it, q).wait_recv()
            for u in range(CUT):
                here = slice(u * unit, (u + 1) * unit)
                y_sum[it, q * CUT + u, me_y] = part[it, q, :, here] + half_recv[it, q, :, here]

        gram = None
        for n in range(units):
            if n < units // 2:
                for k in range(1, Y):
                    crossed(it, n, k).wait_recv()
                value = y_sum[it, n, 0]
                for y in range(1, Y):
                    value = value + y_sum[it, n, y]
                if it > 0:
                    value = value * inv_root
                s_ref[it, n] = value
                remote(
                    BULK, s_ref.at[it, n], s_ref.at[it, units // 2 + n], s_recv_sem.at[it, n], me_r, partner
                ).start()
                gram = square(value) if n == 0 else gram + square(value)
                if n == units // 2 - 1:
                    gsend[it] = gram
                    for k in range(H):
                        h = far(k)
                        gram_copy(it, h, other).start()

                        @pl.when(me_r != base + h)
                        def _():
                            gram_copy(it, h, core).start()

                    grecv[it, 2 * R - 1] = gram
            else:
                landed(s_ref.at[it, n], s_recv_sem.at[it, n - units // 2])
                value = s_ref[it, n]
            high = value.astype(jnp.bfloat16)
            low = (value - high.astype(jnp.float32)).astype(jnp.bfloat16)
            lhs[n % 2, :K, :] = high
            lhs[n % 2, K:, :] = low
            if n < units - 1:
                product = jnp.dot(
                    lhs[n % 2], slab[n * unit : (n + 1) * unit, :], preferred_element_type=jnp.float32
                )
                product = product[:K] + product[K:]
                zacc[...] = product if n == 0 else zacc[...] + product
        for w in range(W):
            cols = slice(w * wave, (w + 1) * wave)
            product = jnp.dot(
                lhs[(units - 1) % 2], slab[(units - 1) * unit :, cols], preferred_element_type=jnp.float32
            )
            product = zacc[:, cols] + product[:K] + product[K:]
            for h in range(H):
                zpart[it, w, h] = product[:, h * bw : (h + 1) * bw]
            for k in range(H):
                z_copy(it, w, far(k)).start()

        if it == 0:
            for i in TASKS[1]:
                turn(i)

        @pl.when(is_owner)
        def _():
            landed(grecv.at[it, pl.ds(0, 2 * R - 1)], g_recv_sem.at[it])
            total = grecv[it, 0]
            for r in range(1, 2 * R):
                total = total + grecv[it, r]
            identity = lax.broadcasted_iota(jnp.int32, (K, LANES), 0) == lax.broadcasted_iota(jnp.int32, (K, LANES), 1)
            inverse = factorize(total, [identity.astype(jnp.float32)])[1][0][:, :K]
            own = me_r - base
            for w in range(W):
                if it == 0 and w == W - 1:
                    for i in TASKS[2]:
                        turn(i)
                landed(zrecv.at[it, w], z_recv_sem.at[it, w])
                total = zrecv[it, w, 0]
                for r in range(1, R):
                    total = total + zrecv[it, w, r]
                block_ref[it, w] = jnp.dot(
                    inverse, total, precision=HIGHEST, preferred_element_type=jnp.float32
                ).astype(jnp.bfloat16)
                for k in range(R):
                    back_copy(it, w, far_row(k), own).start()

        if it == 0:
            @pl.when(jnp.logical_not(is_owner))
            def _():
                for i in TASKS[2]:
                    turn(i)

            for i in TASKS[3]:
                turn(i)

    last = gathered(ITERS - 1)

    def to_partner(k):
        y = lax.rem(me_y + k, Y)
        return remote(BULK, fin_part.at[k], fin_recv.at[k], f_recv_sem.at[k], me_r, partner), y

    for k in list(range(1, Y)) + [0]:
        copy, y = to_partner(k)
        fin_part[k] = last(position(y * 2 + (core if k else other)))
        copy.start()
    for k in list(range(1, Y)) + [0]:
        y = lax.rem(me_y + k, Y)
        fin_send[k] = last(position(y * 2 + (other if k else core)))
    outer = []
    for k in range(1, Y):
        copy, y = to_partner(k)
        copy.wait_recv()
        fin_send[k] = fin_send[k] + fin_recv[k]
        copy = remote(BULK, fin_send.at[k], fin_y.at[k], fy_recv_sem.at[k - 1], me_r, y * 2 + other)
        copy.start()
        outer.append(copy)
    to_partner(0)[0].wait_recv()
    own = fin_send[0] + fin_recv[0]
    for k, copy in enumerate(outer):
        copy.wait_recv()
        own = own + fin_y[k + 1]
    own = own * inv_root
    fsend[...] = square(own)

    n = R * C

    def spread(k):
        pltpu.make_async_remote_copy(
            src_ref=fsend, dst_ref=frecv.at[n - 1 - k], send_sem=send_sem.at[LAST_GRAM],
            recv_sem=c_recv_sem.at[0], device_id=peer(k), device_id_type=MESH,
        ).start()

    repeat(1, n, spread)
    frecv[n - 1] = fsend[...]

    moved = ITERS * (C + Y * (Y - 1) + Y) * K * piece + ITERS * K * width + (2 * Y - 1) * K * piece
    sent_rows(BULK, moved, 4)
    sent(GRAM, frecv.at[pl.ds(0, ITERS * H)])

    @pl.when(is_owner)
    def _():
        sent(OWN_GRAM, frecv.at[pl.ds(0, ITERS * (H - 1))])
        sent_rows(BLOCK, ITERS * W * R * K * bw, 2)

    @pl.when(jnp.logical_not(is_owner))
    def _():
        sent(OWN_GRAM, frecv.at[pl.ds(0, ITERS * H)])

    landed(frecv.at[pl.ds(0, n - 1)], c_recv_sem.at[0])
    def held(d):
        return frecv[lax.rem(d - me - 1 + n, n)]

    parts = [held(d) for d in range(8)]
    for d in range(8, n):
        parts[d % 8] = parts[d % 8] + held(d)
    while len(parts) > 1:
        parts = [a + b for a, b in zip(parts[::2], parts[1::2])]
    chunks = [slice(i, i + LANES) for i in range(0, piece, LANES)]
    upper, ortho = factorize(parts[0], [own[:, chunk] for chunk in chunks])
    for chunk, array in zip(chunks, ortho):
        basis_ref[:, chunk] = array * scale
    factor_ref[...] = upper / scale
    sent(LAST_GRAM, frecv.at[pl.ds(0, n - 1)])


def put_out(basis_ref, factor_ref, basis_out, factor_out, sem):
    copies = [
        pltpu.make_async_copy(basis_ref, basis_out, sem.at[0]),
        pltpu.make_async_copy(factor_ref, factor_out, sem.at[1]),
    ]
    for copy in copies:
        copy.start()
    for copy in copies:
        copy.wait()


def body(affinity, seed_values, sku_ids):
    R, C = lax.axis_size("row"), lax.axis_size("col")
    K = seed_values.shape[0]
    rows, width = affinity.shape
    piece, Y = rows // C, C // 2
    H = min(R // 2, width // LANES)
    W = 4 if width % (4 * H * LANES) == 0 else 1
    base, wave, bw = (R - H) // 2, width // W, width // W // H
    dims = (R, C, K, piece, width, base, H, W, 1.0 / math.sqrt(width * C), math.sqrt(rows * R))
    f32, bf16 = jnp.float32, jnp.bfloat16
    dma = pltpu.SemaphoreType.DMA
    vmem = pl.BlockSpec(memory_space=pltpu.VMEM)
    results = pl.pallas_call(
        functools.partial(kernel, dims),
        out_shape=(
            pltpu.VMEM((K, piece), f32),
            pltpu.VMEM((K, K), f32),
        ),
        in_specs=[pl.BlockSpec(memory_space=pl.ANY)] * 3,
        out_specs=(vmem, vmem),
        scratch_shapes=[
            pltpu.VMEM((rows, width), bf16),
            pltpu.VMEM((C, width, piece), bf16),
            pltpu.SMEM((K,), jnp.int32),
            pltpu.VMEM((1, width), jnp.int32),
            pltpu.VMEM((K, width), bf16),
            pltpu.VMEM((C, K, piece), f32),
            pltpu.VMEM((ITERS, C, K, piece), f32),
            pltpu.VMEM((ITERS, C, K, piece), f32),
            pltpu.VMEM((ITERS, Y * CUT, K, piece // CUT), f32),
            pltpu.VMEM((ITERS, Y * CUT, Y, K, piece // CUT), f32),
            pltpu.VMEM((Y, K, piece), f32),
            pltpu.VMEM((Y, K, piece), f32),
            pltpu.VMEM((Y, K, piece), f32),
            pltpu.VMEM((Y, K, piece), f32),
            pltpu.VMEM((ITERS, C * CUT, K, piece // CUT), f32),
            pltpu.VMEM((2, 2 * K, piece // CUT), bf16),
            pltpu.VMEM((K, width), f32),
            pltpu.VMEM((ITERS, W, H, K, bw), f32),
            pltpu.VMEM((ITERS, W, R, K, bw), f32),
            pltpu.VMEM((ITERS, W, K, bw), bf16),
            pltpu.VMEM((ITERS, W, K, wave), bf16),
            pltpu.VMEM((ITERS, K, K), f32),
            pltpu.VMEM((ITERS, 2 * R, K, K), f32),
            pltpu.VMEM((K, K), f32),
            pltpu.VMEM((R * C, K, K), f32),
            dma((DEPTH + 2,)),
            dma((5,)),
            dma((ITERS, C)),
            dma((ITERS, Y * CUT, Y - 1)),
            dma((Y,)),
            dma((Y - 1,)),
            dma((ITERS, Y * CUT)),
            dma((ITERS, W)),
            dma((ITERS, W)),
            dma((ITERS,)),
            dma((1,)),
        ],
        compiler_params=pltpu.CompilerParams(
            collective_id=0, has_side_effects=True, vmem_limit_bytes=60 * 1024 * 1024
        ),
    )(affinity, seed_values, sku_ids[None, :])
    return pl.pallas_call(
        put_out,
        out_shape=tuple(jax.ShapeDtypeStruct(array.shape, f32) for array in results),
        in_specs=[vmem, vmem],
        out_specs=(pl.BlockSpec(memory_space=pl.ANY),) * 2,
        scratch_shapes=[dma((2,))],
    )(*[pltpu.with_memory_space_constraint(array, pltpu.VMEM) for array in results])


def solution(mesh):
    placed = (P("row", "col"), P(), P("col"))
    return jax.shard_map(
        body, mesh=mesh, in_specs=placed, out_specs=(P(None, ("row", "col")), P()), check_vma=False
    )
```

```python
import functools
import math

import jax
import jax.numpy as jnp
from jax import lax
from jax.experimental import pallas as pl
from jax.experimental.pallas import tpu as pltpu
from jax.sharding import PartitionSpec as P

ITERS = 2
SUB = 2
CUT = 2
DEPTH = 4
LANES = 128
TASKS = ((0, 1), (2, 3, 4), (5,), (6, 7))
HIGHEST = lax.Precision.HIGHEST
MESH = pl.DeviceIdType.MESH

mix_first = -2048144789
mix_second = -1028477387
golden = -1640531535
salt_value = 1540483477


def shifted(value, amount):
    return lax.shift_right_logical(value, jnp.full(value.shape, amount, jnp.int32))


def scramble(value):
    value = jnp.bitwise_xor(value, shifted(value, 16))
    value = value * jnp.int32(mix_first)
    value = jnp.bitwise_xor(value, shifted(value, 13))
    value = value * jnp.int32(mix_second)
    return jnp.bitwise_xor(value, shifted(value, 16))


def test_matrix(seeds, skus, total_columns):
    first = scramble(jnp.bitwise_xor(seeds, skus * jnp.int32(golden)))
    second = scramble(jnp.bitwise_xor(first, jnp.int32(salt_value)))
    uniform_a = (shifted(first, 9) + 1).astype(jnp.float32) / 8388608.0
    uniform_b = (shifted(second, 9) + 1).astype(jnp.float32) / 8388608.0
    gauss = jnp.sqrt(-2.0 * jnp.log(uniform_a)) * jnp.cos(6.283185307179586 * uniform_b)
    return (gauss / math.sqrt(total_columns)).astype(jnp.bfloat16)


def refined_rsqrt(value):
    root = lax.rsqrt(value)
    return root * (1.5 - 0.5 * (value * root) * root)


def factorize(gram, right):
    count = gram.shape[0]
    shape = (count, LANES)
    rows = lax.broadcasted_iota(jnp.int32, shape, 0)
    cols = lax.broadcasted_iota(jnp.int32, shape, 1)
    top = jnp.max(jnp.max(gram, axis=1, keepdims=True), axis=0, keepdims=True)
    scale = refined_rsqrt(top)
    left = jnp.concatenate([gram * (1.0 / top), jnp.zeros((count, LANES - count), jnp.float32)], axis=1)
    arrays = [left] + list(right)
    results = [jnp.zeros(shape, jnp.float32) for _ in arrays]
    for j in range(0, count, 2):
        first = jnp.broadcast_to(arrays[0][:, j : j + 1], shape)
        second = jnp.broadcast_to(arrays[0][:, j + 1 : j + 2], shape)
        a, b, c = first[j : j + 1], first[j + 1 : j + 2], second[j + 1 : j + 2]
        det = a * c - b * b
        inv = 1.0 / det
        below = rows > j + 1
        one = jnp.where(below, first * c - second * b, 0.0) * inv
        two = jnp.where(below, second * a - first * b, 0.0) * inv
        root = refined_rsqrt(a)
        next_root = refined_rsqrt(det) * (a * root)
        ratio = b * root * root
        for i, array in enumerate(arrays):
            head, tail = array[j : j + 1], array[j + 1 : j + 2]
            results[i] = jnp.where(
                rows == j, head * root, jnp.where(rows == j + 1, (tail - ratio * head) * next_root, results[i])
            )
            arrays[i] = array - (one * head + two * tail)
    upper = jnp.where(rows <= cols, results[0], 0.0) * (top * scale)
    return upper[:, :count], [array * scale for array in results[1:]]


def repeat(start, stop, step):
    if stop - start <= 64:
        for k in range(start, stop):
            step(k)
    else:
        lax.fori_loop(start, stop, lambda k, _: (step(k), 0)[1], 0)


def kernel(
    dims,
    slab_hbm, seed_hbm, sku_hbm,
    basis_ref, factor_ref,
    slab, slab_t, seed_ref, sku_ref, x_ref, acc, part, half_recv, y_send, y_sum,
    fin_part, fin_recv, fin_send, fin_y, s_ref, lhs, zacc, zpart, zrecv, block_ref, back,
    gsend, grecv, fsend, frecv,
    load_sem, send_sem, a_recv_sem, y_recv_sem, f_recv_sem, fy_recv_sem, s_recv_sem, z_recv_sem, b_recv_sem,
    g_recv_sem, c_recv_sem,
):
    R, C, K, piece, width, base, H, W, inv_root, scale = dims
    wave = width // W
    bw = wave // H
    me_r = lax.axis_index("row")
    me_c = lax.axis_index("col")
    me = me_r * C + me_c

    Y = C // 2
    core, me_y = lax.rem(me_c, 2), me_c // 2
    other = 1 - core
    partner = me_y * 2 + other

    flip = me_r // (R // 2)
    is_owner = jnp.logical_and(me_r >= base, me_r < base + H)

    def far(k):
        return (H - 1 - k) + flip * (2 * k - H + 1)

    def far_row(k):
        return (R - 1 - k) + flip * (2 * k - R + 1)

    span, unit, units = piece // SUB, piece // CUT, C * CUT
    n_load = C * SUB

    def load(i):
        k = i // SUB
        start = ((other * Y + k) if k < Y else (core * Y + k - Y)) * piece + (i % SUB) * span
        return pltpu.make_async_copy(
            slab_hbm.at[pl.ds(pl.multiple_of(start, span), span), :],
            slab.at[pl.ds(i * span, span), :],
            load_sem.at[i % DEPTH],
        )

    seed_copy = pltpu.make_async_copy(seed_hbm, seed_ref, load_sem.at[DEPTH])
    sku_copy = pltpu.make_async_copy(sku_hbm, sku_ref, load_sem.at[DEPTH + 1])
    seed_copy.start()
    sku_copy.start()
    for i in range(min(DEPTH, n_load)):
        load(i).start()

    def peer(k):
        index = lax.rem(me + k, R * C)
        return {"row": index // C, "col": lax.rem(index, C)}

    barrier = pltpu.get_barrier_semaphore()

    def greet(k):
        pl.semaphore_signal(barrier, inc=1, device_id=peer(k), device_id_type=MESH)

    repeat(1, R * C, greet)

    seed_copy.wait()
    sku_copy.wait()
    index = lax.broadcasted_iota(jnp.int32, (K, width), 0)
    seeds = jnp.zeros((K, width), jnp.int32)
    for k in range(K):
        seeds = jnp.where(index == k, seed_ref[k], seeds)
    x_ref[...] = test_matrix(seeds, jnp.broadcast_to(sku_ref[...], (K, width)), width * C)

    def turn(i):
        here = slice((i % SUB) * span, (i % SUB + 1) * span)
        slab_t[i // SUB, :, here] = slab[i * span : (i + 1) * span, :].T

    BULK, GRAM, OWN_GRAM, BLOCK, LAST_GRAM = range(5)

    def remote(kind, src, dst, recv, row, col):
        return pltpu.make_async_remote_copy(
            src_ref=src, dst_ref=dst, send_sem=send_sem.at[kind], recv_sem=recv,
            device_id={"row": row, "col": col}, device_id_type=MESH,
        )

    def sent(kind, ref):
        remote(kind, ref, ref, send_sem.at[kind], me_r, partner).wait_send()

    def sent_rows(kind, values, itemsize):
        sent(kind, slab.at[pl.ds(0, values * itemsize // (2 * width)), :])

    def position(c):
        half = c // Y
        same = 1 - (half + core - 2 * half * core)
        return lax.rem(c, Y) + Y * same

    def swap(it, slot):
        there = (slot + Y) % C
        return remote(BULK, part.at[it, slot], half_recv.at[it, there], a_recv_sem.at[there], me_r, partner)

    def swapped(it, slot):
        return remote(BULK, part.at[it, slot], half_recv.at[it, slot], a_recv_sem.at[slot], me_r, partner)

    def cross(it, q, k):
        y = lax.rem(me_y + k, Y)
        return remote(
            BULK, y_send.at[it, q], y_sum.at[it, q, me_y], y_recv_sem.at[it, q, k - 1], me_r, y * 2 + other
        )

    def crossed(it, q, k):
        y = lax.rem(me_y + (Y - k), Y)
        return remote(BULK, y_send.at[it, q], y_sum.at[it, q, y], y_recv_sem.at[it, q, k - 1], me_r, partner)

    def square(value):
        return lax.dot_general(
            value, value, (((1,), (1,)), ((), ())), precision=HIGHEST, preferred_element_type=jnp.float32
        )

    def gram_copy(it, h, c):
        slot = lax.rem(me_r * 2 + core - (base + h) * 2 - c - 1 + 4 * R, 2 * R)
        return remote(
            OWN_GRAM if c is core else GRAM, gsend.at[it], grecv.at[it, slot], g_recv_sem.at[it],
            base + h, me_y * 2 + c,
        )

    def z_copy(it, w, h):
        return remote(BULK, zpart.at[it, w, h], zrecv.at[it, w, me_r], z_recv_sem.at[w], base + h, partner)

    def back_copy(it, w, row, h):
        cols = pl.ds(pl.multiple_of(h * bw, bw), bw)
        return remote(BLOCK, block_ref.at[it, w], back.at[it, w, :, cols], b_recv_sem.at[w], row, partner)

    def landed(ref, sem):
        remote(BULK, ref, ref, sem, me_r, partner).wait_recv()

    def gathered(it):
        def product(w, slot):
            rows = slice(w * wave, (w + 1) * wave)
            return jnp.dot(back[it, w], slab_t[slot, rows, :], preferred_element_type=jnp.float32)

        for w in range(W):
            landed(back.at[it, w], b_recv_sem.at[w])
            if w < W - 1:
                for slot in range(C):
                    value = product(w, slot)
                    acc[slot] = value if w == 0 else acc[slot] + value
        if W == 1:
            return lambda slot: product(0, slot)
        return lambda slot: acc[slot] + product(W - 1, slot)

    for it in range(ITERS):
        def hand_over(q):
            swapped(it, Y + q).wait_recv()
            for u in range(CUT):
                here = slice(u * unit, (u + 1) * unit)
                y_send[it, q * CUT + u] = part[it, Y + q, :, here] + half_recv[it, Y + q, :, here]
                for k in range(1, Y):
                    cross(it, q * CUT + u, k).start()

        if it == 0:
            for i in range(n_load):
                k, sub = i // SUB, i % SUB
                here = slice(sub * span, (sub + 1) * span)
                load(i).wait()
                if i + DEPTH < n_load:
                    load(i + DEPTH).start()
                part[it, k, :, here] = lax.dot_general(
                    x_ref[...], slab[i * span : (i + 1) * span, :], (((1,), (1,)), ((), ())), preferred_element_type=jnp.float32
                )
                if i == Y * SUB - 1:
                    pl.semaphore_wait(barrier, R * C - 1)
                    for slot in range(Y):
                        swap(it, slot).start()
                if k >= Y and sub == SUB - 1:
                    swap(it, k).start()
                    hand_over(k - Y)
            for i in TASKS[0]:
                turn(i)
        else:
            last = gathered(it - 1)
            for q in range(Y):
                for slot in (q, Y + q):
                    part[it, slot] = last(slot)
                    swap(it, slot).start()
                    if q > 0 and slot == q:
                        hand_over(q - 1)
            hand_over(Y - 1)
        for q in range(Y):
            swapped(it, q).wait_recv()
            for u in range(CUT):
                here = slice(u * unit, (u + 1) * unit)
                y_sum[it, q * CUT + u, me_y] = part[it, q, :, here] + half_recv[it, q, :, here]

        gram = None
        for n in range(units):
            if n < units // 2:
                for k in range(1, Y):
                    crossed(it, n, k).wait_recv()
                value = y_sum[it, n, 0]
                for y in range(1, Y):
                    value = value + y_sum[it, n, y]
                if it > 0:
                    value = value * inv_root
                s_ref[it, n] = value
                remote(
                    BULK, s_ref.at[it, n], s_ref.at[it, units // 2 + n], s_recv_sem.at[n], me_r, partner
                ).start()
                gram = square(value) if n == 0 else gram + square(value)
                if n == units // 2 - 1:
                    gsend[it] = gram
                    for k in range(H):
                        h = far(k)
                        gram_copy(it, h, other).start()

                        @pl.when(me_r != base + h)
                        def _():
                            gram_copy(it, h, core).start()

                    grecv[it, 2 * R - 1] = gram
            else:
                landed(s_ref.at[it, n], s_recv_sem.at[n - units // 2])
                value = s_ref[it, n]
            high = value.astype(jnp.bfloat16)
            low = (value - high.astype(jnp.float32)).astype(jnp.bfloat16)
            lhs[n % 2, :K, :] = high
            lhs[n % 2, K:, :] = low
            if n < units - 1:
                product = jnp.dot(
                    lhs[n % 2], slab[n * unit : (n + 1) * unit, :], preferred_element_type=jnp.float32
                )
                product = product[:K] + product[K:]
                zacc[...] = product if n == 0 else zacc[...] + product
        for w in range(W):
            cols = slice(w * wave, (w + 1) * wave)
            product = jnp.dot(
                lhs[(units - 1) % 2], slab[(units - 1) * unit :, cols], preferred_element_type=jnp.float32
            )
            product = zacc[:, cols] + product[:K] + product[K:]
            for h in range(H):
                zpart[it, w, h] = product[:, h * bw : (h + 1) * bw]
            for k in range(H):
                z_copy(it, w, far(k)).start()

        if it == 0:
            for i in TASKS[1]:
                turn(i)

        @pl.when(is_owner)
        def _():
            landed(grecv.at[it, pl.ds(0, 2 * R - 1)], g_recv_sem.at[it])
            total = grecv[it, 0]
            for r in range(1, 2 * R):
                total = total + grecv[it, r]
            identity = lax.broadcasted_iota(jnp.int32, (K, LANES), 0) == lax.broadcasted_iota(jnp.int32, (K, LANES), 1)
            inverse = factorize(total, [identity.astype(jnp.float32)])[1][0][:, :K]
            own = me_r - base
            for w in range(W):
                if it == 0 and w == W - 1:
                    for i in TASKS[2]:
                        turn(i)
                landed(zrecv.at[it, w], z_recv_sem.at[w])
                total = zrecv[it, w, 0]
                for r in range(1, R):
                    total = total + zrecv[it, w, r]
                block_ref[it, w] = jnp.dot(
                    inverse, total, precision=HIGHEST, preferred_element_type=jnp.float32
                ).astype(jnp.bfloat16)
                for k in range(R):
                    back_copy(it, w, far_row(k), own).start()

        if it == 0:
            @pl.when(jnp.logical_not(is_owner))
            def _():
                for i in TASKS[2]:
                    turn(i)

            for i in TASKS[3]:
                turn(i)

    last = gathered(ITERS - 1)

    def to_partner(k):
        y = lax.rem(me_y + k, Y)
        return remote(BULK, fin_part.at[k], fin_recv.at[k], f_recv_sem.at[k], me_r, partner), y

    for k in list(range(1, Y)) + [0]:
        copy, y = to_partner(k)
        fin_part[k] = last(position(y * 2 + (core if k else other)))
        copy.start()
    for k in list(range(1, Y)) + [0]:
        y = lax.rem(me_y + k, Y)
        fin_send[k] = last(position(y * 2 + (other if k else core)))
    outer = []
    for k in range(1, Y):
        copy, y = to_partner(k)
        copy.wait_recv()
        fin_send[k] = fin_send[k] + fin_recv[k]
        copy = remote(BULK, fin_send.at[k], fin_y.at[k], fy_recv_sem.at[k - 1], me_r, y * 2 + other)
        copy.start()
        outer.append(copy)
    to_partner(0)[0].wait_recv()
    own = fin_send[0] + fin_recv[0]
    for k, copy in enumerate(outer):
        copy.wait_recv()
        own = own + fin_y[k + 1]
    own = own * inv_root
    fsend[...] = square(own)

    n = R * C

    def spread(k):
        pltpu.make_async_remote_copy(
            src_ref=fsend, dst_ref=frecv.at[n - 1 - k], send_sem=send_sem.at[LAST_GRAM],
            recv_sem=c_recv_sem.at[0], device_id=peer(k), device_id_type=MESH,
        ).start()

    repeat(1, n, spread)
    frecv[n - 1] = fsend[...]

    moved = ITERS * (C + Y * (Y - 1) + Y) * K * piece + ITERS * K * width + (2 * Y - 1) * K * piece
    sent_rows(BULK, moved, 4)
    sent(GRAM, frecv.at[pl.ds(0, ITERS * H)])

    @pl.when(is_owner)
    def _():
        sent(OWN_GRAM, frecv.at[pl.ds(0, ITERS * (H - 1))])
        sent_rows(BLOCK, ITERS * W * R * K * bw, 2)

    @pl.when(jnp.logical_not(is_owner))
    def _():
        sent(OWN_GRAM, frecv.at[pl.ds(0, ITERS * H)])

    landed(frecv.at[pl.ds(0, n - 1)], c_recv_sem.at[0])
    def held(d):
        return frecv[lax.rem(d - me - 1 + n, n)]

    parts = [held(d) for d in range(8)]
    for d in range(8, n):
        parts[d % 8] = parts[d % 8] + held(d)
    while len(parts) > 1:
        parts = [a + b for a, b in zip(parts[::2], parts[1::2])]
    chunks = [slice(i, i + LANES) for i in range(0, piece, LANES)]
    upper, ortho = factorize(parts[0], [own[:, chunk] for chunk in chunks])
    for chunk, array in zip(chunks, ortho):
        basis_ref[:, chunk] = array * scale
    factor_ref[...] = upper / scale
    sent(LAST_GRAM, frecv.at[pl.ds(0, n - 1)])


def put_out(basis_ref, factor_ref, basis_out, factor_out, sem):
    copies = [
        pltpu.make_async_copy(basis_ref, basis_out, sem.at[0]),
        pltpu.make_async_copy(factor_ref, factor_out, sem.at[1]),
    ]
    for copy in copies:
        copy.start()
    for copy in copies:
        copy.wait()


def body(affinity, seed_values, sku_ids):
    R, C = lax.axis_size("row"), lax.axis_size("col")
    K = seed_values.shape[0]
    rows, width = affinity.shape
    piece, Y = rows // C, C // 2
    H = min(R // 2, width // LANES)
    W = 4 if width % (4 * H * LANES) == 0 else 1
    base, wave, bw = (R - H) // 2, width // W, width // W // H
    dims = (R, C, K, piece, width, base, H, W, 1.0 / math.sqrt(width * C), math.sqrt(rows * R))
    f32, bf16 = jnp.float32, jnp.bfloat16
    dma = pltpu.SemaphoreType.DMA
    vmem = pl.BlockSpec(memory_space=pltpu.VMEM)
    results = pl.pallas_call(
        functools.partial(kernel, dims),
        out_shape=(
            pltpu.VMEM((K, piece), f32),
            pltpu.VMEM((K, K), f32),
        ),
        in_specs=[pl.BlockSpec(memory_space=pl.ANY)] * 3,
        out_specs=(vmem, vmem),
        scratch_shapes=[
            pltpu.VMEM((rows, width), bf16),
            pltpu.VMEM((C, width, piece), bf16),
            pltpu.SMEM((K,), jnp.int32),
            pltpu.VMEM((1, width), jnp.int32),
            pltpu.VMEM((K, width), bf16),
            pltpu.VMEM((C, K, piece), f32),
            pltpu.VMEM((ITERS, C, K, piece), f32),
            pltpu.VMEM((ITERS, C, K, piece), f32),
            pltpu.VMEM((ITERS, Y * CUT, K, piece // CUT), f32),
            pltpu.VMEM((ITERS, Y * CUT, Y, K, piece // CUT), f32),
            pltpu.VMEM((Y, K, piece), f32),
            pltpu.VMEM((Y, K, piece), f32),
            pltpu.VMEM((Y, K, piece), f32),
            pltpu.VMEM((Y, K, piece), f32),
            pltpu.VMEM((ITERS, C * CUT, K, piece // CUT), f32),
            pltpu.VMEM((2, 2 * K, piece // CUT), bf16),
            pltpu.VMEM((K, width), f32),
            pltpu.VMEM((ITERS, W, H, K, bw), f32),
            pltpu.VMEM((ITERS, W, R, K, bw), f32),
            pltpu.VMEM((ITERS, W, K, bw), bf16),
            pltpu.VMEM((ITERS, W, K, wave), bf16),
            pltpu.VMEM((ITERS, K, K), f32),
            pltpu.VMEM((ITERS, 2 * R, K, K), f32),
            pltpu.VMEM((K, K), f32),
            pltpu.VMEM((R * C, K, K), f32),
            dma((DEPTH + 2,)),
            dma((5,)),
            dma((C,)),
            dma((ITERS, Y * CUT, Y - 1)),
            dma((Y,)),
            dma((Y - 1,)),
            dma((Y * CUT,)),
            dma((W,)),
            dma((W,)),
            dma((ITERS,)),
            dma((1,)),
        ],
        compiler_params=pltpu.CompilerParams(
            collective_id=0, has_side_effects=True, vmem_limit_bytes=60 * 1024 * 1024
        ),
    )(affinity, seed_values, sku_ids[None, :])
    return pl.pallas_call(
        put_out,
        out_shape=tuple(jax.ShapeDtypeStruct(array.shape, f32) for array in results),
        in_specs=[vmem, vmem],
        out_specs=(pl.BlockSpec(memory_space=pl.ANY),) * 2,
        scratch_shapes=[dma((2,))],
    )(*[pltpu.with_memory_space_constraint(array, pltpu.VMEM) for array in results])


def solution(mesh):
    placed = (P("row", "col"), P(), P("col"))
    return jax.shard_map(
        body, mesh=mesh, in_specs=placed, out_specs=(P(None, ("row", "col")), P()), check_vma=False
    )
```

```python
import functools
import math

import jax
import jax.numpy as jnp
from jax import lax
from jax.experimental import pallas as pl
from jax.experimental.pallas import tpu as pltpu
from jax.sharding import PartitionSpec as P

ITERS = 2
SUB = 2
CUT = 2
DEPTH = 4
LANES = 128
TASKS = ((0, 1), (2, 3, 4), (5,), (6, 7))
HIGHEST = lax.Precision.HIGHEST
MESH = pl.DeviceIdType.MESH

mix_first = -2048144789
mix_second = -1028477387
golden = -1640531535
salt_value = 1540483477


def shifted(value, amount):
    return lax.shift_right_logical(value, jnp.full(value.shape, amount, jnp.int32))


def scramble(value):
    value = jnp.bitwise_xor(value, shifted(value, 16))
    value = value * jnp.int32(mix_first)
    value = jnp.bitwise_xor(value, shifted(value, 13))
    value = value * jnp.int32(mix_second)
    return jnp.bitwise_xor(value, shifted(value, 16))


def test_matrix(seeds, skus, total_columns):
    first = scramble(jnp.bitwise_xor(seeds, skus * jnp.int32(golden)))
    second = scramble(jnp.bitwise_xor(first, jnp.int32(salt_value)))
    uniform_a = (shifted(first, 9) + 1).astype(jnp.float32) / 8388608.0
    uniform_b = (shifted(second, 9) + 1).astype(jnp.float32) / 8388608.0
    gauss = jnp.sqrt(-2.0 * jnp.log(uniform_a)) * jnp.cos(6.283185307179586 * uniform_b)
    return (gauss / math.sqrt(total_columns)).astype(jnp.bfloat16)


def refined_rsqrt(value):
    root = lax.rsqrt(value)
    return root * (1.5 - 0.5 * (value * root) * root)


def factorize(gram, right):
    count = gram.shape[0]
    shape = (count, LANES)
    rows = lax.broadcasted_iota(jnp.int32, shape, 0)
    cols = lax.broadcasted_iota(jnp.int32, shape, 1)
    top = jnp.max(jnp.max(gram, axis=1, keepdims=True), axis=0, keepdims=True)
    scale = refined_rsqrt(top)
    left = jnp.concatenate([gram * (1.0 / top), jnp.zeros((count, LANES - count), jnp.float32)], axis=1)
    arrays = [left] + list(right)
    results = [jnp.zeros(shape, jnp.float32) for _ in arrays]
    for j in range(0, count, 2):
        first = jnp.broadcast_to(arrays[0][:, j : j + 1], shape)
        second = jnp.broadcast_to(arrays[0][:, j + 1 : j + 2], shape)
        a, b, c = first[j : j + 1], first[j + 1 : j + 2], second[j + 1 : j + 2]
        det = a * c - b * b
        inv = 1.0 / det
        below = rows > j + 1
        one = jnp.where(below, first * c - second * b, 0.0) * inv
        two = jnp.where(below, second * a - first * b, 0.0) * inv
        root = refined_rsqrt(a)
        next_root = refined_rsqrt(det) * (a * root)
        ratio = b * root * root
        for i, array in enumerate(arrays):
            head, tail = array[j : j + 1], array[j + 1 : j + 2]
            results[i] = jnp.where(
                rows == j, head * root, jnp.where(rows == j + 1, (tail - ratio * head) * next_root, results[i])
            )
            arrays[i] = array - (one * head + two * tail)
    upper = jnp.where(rows <= cols, results[0], 0.0) * (top * scale)
    return upper[:, :count], [array * scale for array in results[1:]]


def repeat(start, stop, step):
    if stop - start <= 64:
        for k in range(start, stop):
            step(k)
    else:
        lax.fori_loop(start, stop, lambda k, _: (step(k), 0)[1], 0)


def kernel(
    dims,
    slab_hbm, seed_hbm, sku_hbm,
    basis_ref, factor_ref,
    slab, slab_t, seed_ref, sku_ref, x_ref, acc, part, half_recv, y_send, y_sum,
    fin_part, fin_recv, fin_send, fin_y, s_ref, lhs, zacc, zpart, zrecv, block_ref, back,
    gsend, grecv, fsend, frecv,
    load_sem, send_sem, a_recv_sem, y_recv_sem, f_recv_sem, fy_recv_sem, s_recv_sem, z_recv_sem, b_recv_sem,
    g_recv_sem, c_recv_sem,
):
    R, C, K, piece, width, base, H, W, inv_root, scale = dims
    wave = width // W
    bw = wave // H
    me_r = lax.axis_index("row")
    me_c = lax.axis_index("col")
    me = me_r * C + me_c

    Y = C // 2
    core, me_y = lax.rem(me_c, 2), me_c // 2
    other = 1 - core
    partner = me_y * 2 + other

    flip = me_r // (R // 2)
    is_owner = jnp.logical_and(me_r >= base, me_r < base + H)

    def far(k):
        return (H - 1 - k) + flip * (2 * k - H + 1)

    def far_row(k):
        return (R - 1 - k) + flip * (2 * k - R + 1)

    span, unit, units = piece // SUB, piece // CUT, C * CUT
    n_load = C * SUB

    def load(i):
        k = i // SUB
        start = ((other * Y + k) if k < Y else (core * Y + k - Y)) * piece + (i % SUB) * span
        return pltpu.make_async_copy(
            slab_hbm.at[pl.ds(pl.multiple_of(start, span), span), :],
            slab.at[pl.ds(i * span, span), :],
            load_sem.at[i % DEPTH],
        )

    seed_copy = pltpu.make_async_copy(seed_hbm, seed_ref, load_sem.at[DEPTH])
    sku_copy = pltpu.make_async_copy(sku_hbm, sku_ref, load_sem.at[DEPTH + 1])
    seed_copy.start()
    sku_copy.start()
    for i in range(min(DEPTH, n_load)):
        load(i).start()

    def peer(k):
        index = lax.rem(me + k, R * C)
        return {"row": index // C, "col": lax.rem(index, C)}

    barrier = pltpu.get_barrier_semaphore()

    def greet(k):
        pl.semaphore_signal(barrier, inc=1, device_id=peer(k), device_id_type=MESH)

    repeat(1, R * C, greet)

    seed_copy.wait()
    sku_copy.wait()
    index = lax.broadcasted_iota(jnp.int32, (K, width), 0)
    seeds = jnp.zeros((K, width), jnp.int32)
    for k in range(K):
        seeds = jnp.where(index == k, seed_ref[k], seeds)
    x_ref[...] = test_matrix(seeds, jnp.broadcast_to(sku_ref[...], (K, width)), width * C)

    def turn(i):
        here = slice((i % SUB) * span, (i % SUB + 1) * span)
        slab_t[i // SUB, :, here] = slab[i * span : (i + 1) * span, :].T

    BULK, GRAM, OWN_GRAM, BLOCK, LAST_GRAM = range(5)

    def remote(kind, src, dst, recv, row, col):
        return pltpu.make_async_remote_copy(
            src_ref=src, dst_ref=dst, send_sem=send_sem.at[kind], recv_sem=recv,
            device_id={"row": row, "col": col}, device_id_type=MESH,
        )

    def sent(kind, ref):
        remote(kind, ref, ref, send_sem.at[kind], me_r, partner).wait_send()

    def sent_rows(kind, values, itemsize):
        sent(kind, slab.at[pl.ds(0, values * itemsize // (2 * width)), :])

    def position(c):
        half = c // Y
        same = 1 - (half + core - 2 * half * core)
        return lax.rem(c, Y) + Y * same

    def swap(it, slot):
        there = (slot + Y) % C
        return remote(BULK, part.at[it, slot], half_recv.at[it, there], a_recv_sem.at[there], me_r, partner)

    def swapped(it, slot):
        return remote(BULK, part.at[it, slot], half_recv.at[it, slot], a_recv_sem.at[slot], me_r, partner)

    def cross(it, q, k):
        y = lax.rem(me_y + k, Y)
        return remote(
            BULK, y_send.at[it, q], y_sum.at[it, q, me_y], y_recv_sem.at[it, q, k - 1], me_r, y * 2 + other
        )

    def crossed(it, q, k):
        y = lax.rem(me_y + (Y - k), Y)
        return remote(BULK, y_send.at[it, q], y_sum.at[it, q, y], y_recv_sem.at[it, q, k - 1], me_r, partner)

    def square(value):
        return lax.dot_general(
            value, value, (((1,), (1,)), ((), ())), precision=HIGHEST, preferred_element_type=jnp.float32
        )

    def gram_copy(it, h, c):
        slot = lax.rem(me_r * 2 + core - (base + h) * 2 - c - 1 + 4 * R, 2 * R)
        return remote(
            OWN_GRAM if c is core else GRAM, gsend.at[it], grecv.at[it, slot], g_recv_sem.at[it],
            base + h, me_y * 2 + c,
        )

    def z_copy(it, w, h):
        return remote(BULK, zpart.at[it, w, h], zrecv.at[it, w, me_r], z_recv_sem.at[w], base + h, partner)

    def back_copy(it, w, row, h):
        cols = pl.ds(pl.multiple_of(h * bw, bw), bw)
        return remote(BLOCK, block_ref.at[it, w], back.at[it, w, :, cols], b_recv_sem.at[w], row, partner)

    def landed(ref, sem):
        remote(BULK, ref, ref, sem, me_r, partner).wait_recv()

    def gathered(it):
        def product(w, slot):
            rows = slice(w * wave, (w + 1) * wave)
            return jnp.dot(back[it, w], slab_t[slot, rows, :], preferred_element_type=jnp.float32)

        for w in range(W):
            landed(back.at[it, w], b_recv_sem.at[w])
            if w < W - 1:
                for slot in range(C):
                    value = product(w, slot)
                    acc[slot] = value if w == 0 else acc[slot] + value
        if W == 1:
            return lambda slot: product(0, slot)
        return lambda slot: acc[slot] + product(W - 1, slot)

    for it in range(ITERS):
        def hand_over(q):
            swapped(it, Y + q).wait_recv()
            for u in range(CUT):
                here = slice(u * unit, (u + 1) * unit)
                y_send[it, q * CUT + u] = part[it, Y + q, :, here] + half_recv[it, Y + q, :, here]
                for k in range(1, Y):
                    cross(it, q * CUT + u, k).start()

        if it == 0:
            for i in range(n_load):
                k, sub = i // SUB, i % SUB
                here = slice(sub * span, (sub + 1) * span)
                load(i).wait()
                if i + DEPTH < n_load:
                    load(i + DEPTH).start()
                part[it, k, :, here] = lax.dot_general(
                    x_ref[...], slab[i * span : (i + 1) * span, :], (((1,), (1,)), ((), ())), preferred_element_type=jnp.float32
                )
                if i == Y * SUB - 1:
                    pl.semaphore_wait(barrier, R * C - 1)
                    for slot in range(Y):
                        swap(it, slot).start()
                if k >= Y and sub == SUB - 1:
                    swap(it, k).start()
                    hand_over(k - Y)
            for i in TASKS[0]:
                turn(i)
        else:
            last = gathered(it - 1)
            for q in range(Y):
                for slot in (q, Y + q):
                    part[it, slot] = last(slot)
                    swap(it, slot).start()
                    if q > 0 and slot == q:
                        hand_over(q - 1)
            hand_over(Y - 1)
        for q in range(Y):
            swapped(it, q).wait_recv()
            for u in range(CUT):
                here = slice(u * unit, (u + 1) * unit)
                y_sum[it, q * CUT + u, me_y] = part[it, q, :, here] + half_recv[it, q, :, here]

        gram = None
        for n in range(units):
            if n < units // 2:
                for k in range(1, Y):
                    crossed(it, n, k).wait_recv()
                value = y_sum[it, n, 0]
                for y in range(1, Y):
                    value = value + y_sum[it, n, y]
                if it > 0:
                    value = value * inv_root
                s_ref[it, n] = value
                remote(
                    BULK, s_ref.at[it, n], s_ref.at[it, units // 2 + n], s_recv_sem.at[n], me_r, partner
                ).start()
                gram = square(value) if n == 0 else gram + square(value)
                if n == units // 2 - 1:
                    gsend[it] = gram
                    for k in range(H):
                        h = far(k)
                        gram_copy(it, h, other).start()

                        @pl.when(me_r != base + h)
                        def _():
                            gram_copy(it, h, core).start()

                    grecv[it, 2 * R - 1] = gram
            else:
                landed(s_ref.at[it, n], s_recv_sem.at[n - units // 2])
                value = s_ref[it, n]
            high = value.astype(jnp.bfloat16)
            low = (value - high.astype(jnp.float32)).astype(jnp.bfloat16)
            lhs[n % 2, :K, :] = high
            lhs[n % 2, K:, :] = low
            if n < units - 1:
                product = jnp.dot(
                    lhs[n % 2], slab[n * unit : (n + 1) * unit, :], preferred_element_type=jnp.float32
                )
                product = product[:K] + product[K:]
                zacc[...] = product if n == 0 else zacc[...] + product
        for w in range(W):
            cols = slice(w * wave, (w + 1) * wave)
            product = jnp.dot(
                lhs[(units - 1) % 2], slab[(units - 1) * unit :, cols], preferred_element_type=jnp.float32
            )
            product = zacc[:, cols] + product[:K] + product[K:]
            for h in range(H):
                zpart[it, w, h] = product[:, h * bw : (h + 1) * bw]
            for k in range(H):
                z_copy(it, w, far(k)).start()

        if it == 0:
            for i in TASKS[1]:
                turn(i)

        @pl.when(is_owner)
        def _():
            landed(grecv.at[it, pl.ds(0, 2 * R - 1)], g_recv_sem.at[it])
            total = grecv[it, 0]
            for r in range(1, 2 * R):
                total = total + grecv[it, r]
            identity = lax.broadcasted_iota(jnp.int32, (K, LANES), 0) == lax.broadcasted_iota(jnp.int32, (K, LANES), 1)
            inverse = factorize(total, [identity.astype(jnp.float32)])[1][0][:, :K]
            own = me_r - base
            for w in range(W):
                if it == 0 and w == W - 1:
                    for i in TASKS[2]:
                        turn(i)
                landed(zrecv.at[it, w], z_recv_sem.at[w])
                total = zrecv[it, w, 0]
                for r in range(1, R):
                    total = total + zrecv[it, w, r]
                block_ref[it, w] = jnp.dot(
                    inverse, total, precision=HIGHEST, preferred_element_type=jnp.float32
                ).astype(jnp.bfloat16)
                for k in range(R):
                    back_copy(it, w, far_row(k), own).start()

        if it == 0:
            @pl.when(jnp.logical_not(is_owner))
            def _():
                for i in TASKS[2]:
                    turn(i)

            for i in TASKS[3]:
                turn(i)

    last = gathered(ITERS - 1)

    def to_partner(k):
        y = lax.rem(me_y + k, Y)
        return remote(BULK, fin_part.at[k], fin_recv.at[k], f_recv_sem.at[k], me_r, partner), y

    for k in list(range(1, Y)) + [0]:
        copy, y = to_partner(k)
        fin_part[k] = last(position(y * 2 + (core if k else other)))
        copy.start()
    for k in list(range(1, Y)) + [0]:
        y = lax.rem(me_y + k, Y)
        fin_send[k] = last(position(y * 2 + (other if k else core)))
    outer = []
    for k in range(1, Y):
        copy, y = to_partner(k)
        copy.wait_recv()
        fin_send[k] = fin_send[k] + fin_recv[k]
        copy = remote(BULK, fin_send.at[k], fin_y.at[k], fy_recv_sem.at[k - 1], me_r, y * 2 + other)
        copy.start()
        outer.append(copy)
    to_partner(0)[0].wait_recv()
    own = fin_send[0] + fin_recv[0]
    for k, copy in enumerate(outer):
        copy.wait_recv()
        own = own + fin_y[k + 1]
    own = own * inv_root
    fsend[...] = square(own)

    n = R * C

    def spread(k):
        pltpu.make_async_remote_copy(
            src_ref=fsend, dst_ref=frecv.at[n - 1 - k], send_sem=send_sem.at[LAST_GRAM],
            recv_sem=c_recv_sem.at[0], device_id=peer(k), device_id_type=MESH,
        ).start()

    repeat(1, n, lambda k: spread(n - k))
    frecv[n - 1] = fsend[...]

    moved = ITERS * (C + Y * (Y - 1) + Y) * K * piece + ITERS * K * width + (2 * Y - 1) * K * piece
    sent_rows(BULK, moved, 4)
    sent(GRAM, frecv.at[pl.ds(0, ITERS * H)])

    @pl.when(is_owner)
    def _():
        sent(OWN_GRAM, frecv.at[pl.ds(0, ITERS * (H - 1))])
        sent_rows(BLOCK, ITERS * W * R * K * bw, 2)

    @pl.when(jnp.logical_not(is_owner))
    def _():
        sent(OWN_GRAM, frecv.at[pl.ds(0, ITERS * H)])

    landed(frecv.at[pl.ds(0, n - 1)], c_recv_sem.at[0])
    def held(d):
        return frecv[lax.rem(d - me - 1 + n, n)]

    parts = [held(d) for d in range(8)]
    for d in range(8, n):
        parts[d % 8] = parts[d % 8] + held(d)
    while len(parts) > 1:
        parts = [a + b for a, b in zip(parts[::2], parts[1::2])]
    chunks = [slice(i, i + LANES) for i in range(0, piece, LANES)]
    upper, ortho = factorize(parts[0], [own[:, chunk] for chunk in chunks])
    for chunk, array in zip(chunks, ortho):
        basis_ref[:, chunk] = array * scale
    factor_ref[...] = upper / scale
    sent(LAST_GRAM, frecv.at[pl.ds(0, n - 1)])


def put_out(basis_ref, factor_ref, basis_out, factor_out, sem):
    copies = [
        pltpu.make_async_copy(basis_ref, basis_out, sem.at[0]),
        pltpu.make_async_copy(factor_ref, factor_out, sem.at[1]),
    ]
    for copy in copies:
        copy.start()
    for copy in copies:
        copy.wait()


def body(affinity, seed_values, sku_ids):
    R, C = lax.axis_size("row"), lax.axis_size("col")
    K = seed_values.shape[0]
    rows, width = affinity.shape
    piece, Y = rows // C, C // 2
    H = min(R // 2, width // LANES)
    W = 4 if width % (4 * H * LANES) == 0 else 1
    base, wave, bw = (R - H) // 2, width // W, width // W // H
    dims = (R, C, K, piece, width, base, H, W, 1.0 / math.sqrt(width * C), math.sqrt(rows * R))
    f32, bf16 = jnp.float32, jnp.bfloat16
    dma = pltpu.SemaphoreType.DMA
    vmem = pl.BlockSpec(memory_space=pltpu.VMEM)
    results = pl.pallas_call(
        functools.partial(kernel, dims),
        out_shape=(
            pltpu.VMEM((K, piece), f32),
            pltpu.VMEM((K, K), f32),
        ),
        in_specs=[pl.BlockSpec(memory_space=pl.ANY)] * 3,
        out_specs=(vmem, vmem),
        scratch_shapes=[
            pltpu.VMEM((rows, width), bf16),
            pltpu.VMEM((C, width, piece), bf16),
            pltpu.SMEM((K,), jnp.int32),
            pltpu.VMEM((1, width), jnp.int32),
            pltpu.VMEM((K, width), bf16),
            pltpu.VMEM((C, K, piece), f32),
            pltpu.VMEM((ITERS, C, K, piece), f32),
            pltpu.VMEM((ITERS, C, K, piece), f32),
            pltpu.VMEM((ITERS, Y * CUT, K, piece // CUT), f32),
            pltpu.VMEM((ITERS, Y * CUT, Y, K, piece // CUT), f32),
            pltpu.VMEM((Y, K, piece), f32),
            pltpu.VMEM((Y, K, piece), f32),
            pltpu.VMEM((Y, K, piece), f32),
            pltpu.VMEM((Y, K, piece), f32),
            pltpu.VMEM((ITERS, C * CUT, K, piece // CUT), f32),
            pltpu.VMEM((2, 2 * K, piece // CUT), bf16),
            pltpu.VMEM((K, width), f32),
            pltpu.VMEM((ITERS, W, H, K, bw), f32),
            pltpu.VMEM((ITERS, W, R, K, bw), f32),
            pltpu.VMEM((ITERS, W, K, bw), bf16),
            pltpu.VMEM((ITERS, W, K, wave), bf16),
            pltpu.VMEM((ITERS, K, K), f32),
            pltpu.VMEM((ITERS, 2 * R, K, K), f32),
            pltpu.VMEM((K, K), f32),
            pltpu.VMEM((R * C, K, K), f32),
            dma((DEPTH + 2,)),
            dma((5,)),
            dma((C,)),
            dma((ITERS, Y * CUT, Y - 1)),
            dma((Y,)),
            dma((Y - 1,)),
            dma((Y * CUT,)),
            dma((W,)),
            dma((W,)),
            dma((ITERS,)),
            dma((1,)),
        ],
        compiler_params=pltpu.CompilerParams(
            collective_id=0, has_side_effects=True, vmem_limit_bytes=60 * 1024 * 1024
        ),
    )(affinity, seed_values, sku_ids[None, :])
    return pl.pallas_call(
        put_out,
        out_shape=tuple(jax.ShapeDtypeStruct(array.shape, f32) for array in results),
        in_specs=[vmem, vmem],
        out_specs=(pl.BlockSpec(memory_space=pl.ANY),) * 2,
        scratch_shapes=[dma((2,))],
    )(*[pltpu.with_memory_space_constraint(array, pltpu.VMEM) for array in results])


def solution(mesh):
    placed = (P("row", "col"), P(), P("col"))
    return jax.shard_map(
        body, mesh=mesh, in_specs=placed, out_specs=(P(None, ("row", "col")), P()), check_vma=False
    )
```
